32 devices in a mesh: cls: 8 (over y, x, core), batch: 4 (over z).
Axes of the slice: x: 2, y: 2, z: 4, core: 2. Of those that a mesh axis runs over, the one named last changes fastest.
Arguments:
- features: bfloat16 [4096, 1024], P('batch'), may hold values from -6 to 6
- head_weight: bfloat16 [1024, 1024], P('cls'), may hold values from -0.1875 to 0.1875
- inliers: bfloat16 [8192, 1024], P('cls'), may hold values from -2.5 to 2.5
- outliers: bfloat16 [8192, 1024], P('cls'), may hold values from -2.5 to 2.5
- inlier_counts: int32 [8192], P('cls'), may hold values from 1 to 9
- outlier_counts: int32 [8192], P('cls'), may hold values from 1 to 9
- labels: int32 [4096], P('batch'), may hold values from 0 to 1
Outputs:
- energy: float32 [4096], P('batch')
- head_grad: float32 [1024, 1024], P('cls')
The draws below stay inside these ranges and needn't reach their ends.
All inputs are finite; a program needn't handle non-finite values.
Results may differ from the reference program's by a relative error of at most 0.0076.
The reference program's roundings to bfloat16 on the way (of `queries`) count: a program that leaves them out, or rounds other values in their place, can miss the bound.
Values may be sent and summed in bfloat16 or wider, within the bound.
No kernel may reach another device: no remote copies, remote signals or barrier semaphores. Data moves between devices by JAX's collectives and lax.ppermute only.
A program may use at most 64 MiB of HBM per device.

```python
import math
import jax
import jax.numpy as jnp
from jax import lax

D = 1024
F = 1024
INLIERS = 8192
OUTLIERS = 8192
QUERIES = 4096


def pattern_draw(key, rows):
    scale = 1.0 / math.sqrt(D)
    values = jax.random.normal(key, (rows, D), jnp.float32)
    values = jnp.clip(values * scale, -2.5, 2.5)
    return values.astype(jnp.bfloat16)


def draw_inliers(key, part):
    return pattern_draw(jax.random.fold_in(key, 11), INLIERS)


def draw_outliers(key, part):
    return pattern_draw(jax.random.fold_in(key, 23), OUTLIERS)


def place_ends(entries, key, low, largest):
    index_at = [jax.random.randint(jax.random.fold_in(key, axis), (), 0, length) for axis, length in enumerate(entries.shape)]
    main_axis = entries.shape.index(max(entries.shape))
    beside = index_at[:main_axis] + [(index_at[main_axis] + 1) % entries.shape[main_axis]] + index_at[main_axis + 1:]
    return entries.at[tuple(index_at)].set(low).at[tuple(beside)].set(largest)


def block_scale(stream_key, extent, cuts, smallest, largest):
    gain, own = 1.0, jax.random.fold_in(stream_key, 6)
    for dim, blocks in cuts:
        steps = jnp.exp(jax.random.uniform(jax.random.fold_in(own, dim), (blocks,), jnp.float32, smallest / len(cuts), largest / len(cuts)))
        gain = gain * jnp.repeat(steps, extent[dim] // blocks).reshape([-1 if axis == dim else 1 for axis in range(len(extent))])
    return gain


def gaussian(key, extent, width, limit, shards=(), dtype=jnp.bfloat16):
    entries = width * jax.random.normal(key, extent, jnp.float32)
    if shards:
        entries = entries * block_scale(key, extent, shards, -0.22, 0.18)
    return jnp.clip(entries, -limit, limit).astype(dtype)


def setup_inputs(seed: int = 0) -> dict:
    seeds = jax.random.split(jax.random.key(seed), 8)
    features = gaussian(seeds[0], (QUERIES, F), 1.0, 6.0, ((0, 4),))
    head_weight = gaussian(seeds[1], (F, D), F ** -0.5, 0.1875, ((0, 8),))
    inliers = draw_inliers(jax.random.fold_in(seeds[7], 71), 0)
    outliers = draw_outliers(jax.random.fold_in(seeds[7], 71), 0)
    inlier_counts = place_ends(jax.random.randint(seeds[4], (INLIERS,), 1, 10), jax.random.fold_in(seeds[4], 1), 1, 9).astype(jnp.int32)
    outlier_counts = place_ends(jax.random.randint(seeds[5], (OUTLIERS,), 1, 10), jax.random.fold_in(seeds[5], 1), 1, 9).astype(jnp.int32)
    labels = place_ends(jax.random.randint(seeds[6], (QUERIES,), 0, 2), jax.random.fold_in(seeds[6], 1), 0, 1).astype(jnp.int32)
    return dict(features=features, head_weight=head_weight, inliers=inliers, outliers=outliers, inlier_counts=inlier_counts, outlier_counts=outlier_counts, labels=labels)


beta = 2.0


def retrieve(query_block, patterns, log_counts):
    scores = beta * jnp.dot(query_block, patterns.T, preferred_element_type=jnp.float32) + log_counts[None, :]
    top_score = jnp.max(scores, axis=1)
    expon = jnp.exp(scores - top_score[:, None])
    total = jnp.sum(expon, axis=1)
    weighted = jnp.dot(expon.astype(jnp.bfloat16), patterns, preferred_element_type=jnp.float32)
    return top_score, total, weighted


def reference(features, head_weight, inliers, outliers, inlier_counts, outlier_counts, labels):
    queries = jnp.dot(features, head_weight, preferred_element_type=jnp.float32).astype(jnp.bfloat16)
    in_logs = jnp.log(inlier_counts.astype(jnp.float32))
    out_logs = jnp.log(outlier_counts.astype(jnp.float32))
    block_rows = math.gcd(QUERIES, 256)
    blocks = queries.reshape(QUERIES // block_rows, block_rows, D)

    def per_block(query_block):
        in_top, in_total, in_sum = retrieve(query_block, inliers, in_logs)
        out_top, out_total, out_sum = retrieve(query_block, outliers, out_logs)
        return in_top, in_total, in_sum, out_top, out_total, out_sum

    in_top, in_total, in_sum, out_top, out_total, out_sum = lax.map(per_block, blocks)
    in_top = in_top.reshape(QUERIES)
    in_total = in_total.reshape(QUERIES)
    out_top = out_top.reshape(QUERIES)
    out_total = out_total.reshape(QUERIES)
    in_sum = in_sum.reshape(QUERIES, D)
    out_sum = out_sum.reshape(QUERIES, D)
    energy = ((in_top + jnp.log(in_total)) - (out_top + jnp.log(out_total))) / beta
    label_sign = 2.0 * labels.astype(jnp.float32) - 1.0
    slope_term = -label_sign * jax.nn.sigmoid(-label_sign * energy)
    query_grad = slope_term[:, None] * (in_sum / in_total[:, None] - out_sum / out_total[:, None])
    head_grad = jnp.dot(features.astype(jnp.float32).T, query_grad, precision=lax.Precision.HIGHEST)
    return energy, head_grad
```

```python
import functools

import jax
import jax.numpy as jnp
from jax import lax
from jax.experimental import pallas as pl
from jax.experimental.pallas import tpu as pltpu
from jax.sharding import PartitionSpec as P

beta = 2.0
BF = jnp.bfloat16
F32 = jnp.float32


def orders(bits):
    turn = len(bits) // 2
    return bits, bits[turn:] + bits[:turn]


def gather_masks(order):
    masks = [0, 1]
    for bit in order:
        masks = masks + [mask ^ (1 << bit) for mask in masks]
    return masks


def scatter_masks(order):
    masks = [0]
    for bit in reversed(order):
        masks = [mask ^ (1 << bit) for mask in masks] + masks
    return masks


def by_core(core, first, second):
    return jnp.where(core == 0, jnp.array(first, jnp.int32), jnp.array(second, jnp.int32))


def cls_swap(value, n, bit_of):
    return lax.ppermute(value, "cls", [(i, i ^ (1 << bit_of[i & 1])) for i in range(n)])


def batch_swap(value, n, depth, bit_of):
    pairs = []
    for i in range(n):
        for j in range(depth):
            pairs.append((i * depth + j, i * depth + (j ^ (1 << bit_of[i & 1]))))
    return lax.ppermute(value, ("cls", "batch"), pairs)


def turn_kernel(place_ref, features_ref, out_ref, turned_ref, *, n, rows):
    turned_ref[...] = features_ref[...].T
    for p in range(n):
        start = pl.multiple_of(place_ref[p] * rows, rows)
        out_ref[p * rows:(p + 1) * rows, :] = turned_ref[pl.ds(start, rows), :]


def turn_features(features, place, n):
    q, f = features.shape
    return pl.pallas_call(
        functools.partial(turn_kernel, n=n, rows=f // n),
        out_shape=jax.ShapeDtypeStruct((f, q), BF),
        in_specs=[pl.BlockSpec(memory_space=pltpu.SMEM), pl.BlockSpec(memory_space=pltpu.VMEM)],
        out_specs=pl.BlockSpec(memory_space=pltpu.VMEM),
        scratch_shapes=[pltpu.VMEM((f, q), BF)],
        compiler_params=pltpu.CompilerParams(vmem_limit_bytes=16 << 20),
        cost_estimate=pl.CostEstimate(flops=0, bytes_accessed=8 * q * f, transcendentals=0),
        name="turn",
    )(place, features)


def query_kernel(place_ref, features_ref, blocks_ref, out_ref, weight_ref, *, n, rows, tile):
    for p in range(n):
        start = pl.multiple_of(place_ref[p] * rows, rows)
        weight_ref[pl.ds(start, rows), :] = blocks_ref[p * rows:(p + 1) * rows, :]
    total = features_ref.shape[0]

    @pl.loop(0, total // tile)
    def _(i):
        part = pl.ds(pl.multiple_of(i * tile, tile), tile)
        out_ref[part, :] = jnp.dot(
            features_ref[part, :], weight_ref[...], preferred_element_type=F32
        ).astype(BF)


def half_queries(features, blocks, place, n):
    q, f = features.shape
    width = blocks.shape[1]
    return pl.pallas_call(
        functools.partial(query_kernel, n=n, rows=f // n, tile=256),
        out_shape=jax.ShapeDtypeStruct((q, width), BF),
        in_specs=[pl.BlockSpec(memory_space=pltpu.SMEM)] + [pl.BlockSpec(memory_space=pltpu.VMEM)] * 2,
        out_specs=pl.BlockSpec(memory_space=pltpu.VMEM),
        scratch_shapes=[pltpu.VMEM((f, width), BF)],
        compiler_params=pltpu.CompilerParams(vmem_limit_bytes=16 << 20),
        cost_estimate=pl.CostEstimate(flops=2 * q * f * width, bytes_accessed=4 * q * f, transcendentals=0),
        name="queries",
    )(place, features, blocks)


def to_rows(columns, width):
    r = columns[0].shape[0]
    lane = lax.broadcasted_iota(jnp.int32, (r, width), 1)
    mixed = jnp.broadcast_to(columns[0], (r, width))
    for i, column in enumerate(columns[1:], 1):
        mixed = jnp.where(lane == i, column, mixed)
    return mixed.T[: len(columns), :]


def score_kernel(core_ref, mine_ref, other_ref, in_ref, out_ref, in_counts_ref, out_counts_ref,
                 in_weights_ref, out_weights_ref, stats_ref, query_ref):
    half = mine_ref.shape[1]
    core = core_ref[0]
    query_ref[:, pl.ds(pl.multiple_of(core * half, half), half)] = mine_ref[...] * beta
    query_ref[:, pl.ds(pl.multiple_of((1 - core) * half, half), half)] = other_ref[...] * beta
    stats = []
    for patterns_ref, counts_ref, weights_ref in (
        (in_ref, in_counts_ref, in_weights_ref),
        (out_ref, out_counts_ref, out_weights_ref),
    ):
        scores = lax.dot_general(
            query_ref[...], patterns_ref[...], (((1,), (1,)), ((), ())), preferred_element_type=F32
        ) + jnp.log(counts_ref[...].astype(F32))
        top = jnp.max(scores, axis=1, keepdims=True)
        expon = jnp.exp(scores - top)
        weights_ref[...] = expon.astype(BF)
        stats += [top, jnp.sum(expon, axis=1, keepdims=True)]
    stats_ref[...] = to_rows(stats, 128)


def local_weights(core, mine, other, inliers, outliers, in_counts, out_counts):
    q, half = mine.shape
    d = inliers.shape[1]
    tile = 256
    row = lambda i, *_: (i, 0)
    whole = lambda i, *_: (0, 0)
    ins, outs = inliers.shape[0], outliers.shape[0]
    return pl.pallas_call(
        score_kernel,
        out_shape=(
            jax.ShapeDtypeStruct((q, ins), BF),
            jax.ShapeDtypeStruct((q, outs), BF),
            jax.ShapeDtypeStruct((4, q), F32),
        ),
        grid_spec=pltpu.PrefetchScalarGridSpec(
            num_scalar_prefetch=1,
            grid=(q // tile,),
            in_specs=[
                pl.BlockSpec((tile, half), row),
                pl.BlockSpec((tile, half), row),
                pl.BlockSpec((ins, d), whole),
                pl.BlockSpec((outs, d), whole),
                pl.BlockSpec((1, ins), whole),
                pl.BlockSpec((1, outs), whole),
            ],
            out_specs=[
                pl.BlockSpec((tile, ins), row),
                pl.BlockSpec((tile, outs), row),
                pl.BlockSpec((4, tile), lambda i, *_: (0, i)),
            ],
            scratch_shapes=[pltpu.VMEM((tile, d), BF)],
        ),
        compiler_params=pltpu.CompilerParams(vmem_limit_bytes=32 << 20),
        cost_estimate=pl.CostEstimate(
            flops=2 * q * d * (ins + outs), bytes_accessed=2 * d * (ins + outs), transcendentals=q * (ins + outs)
        ),
        name="scores",
    )(core, mine, other, inliers, outliers, in_counts, out_counts)


def merge(mine, other):
    rows = []
    for i in (0, 2):
        top = jnp.maximum(mine[i], other[i])
        rows += [top, mine[i + 1] * jnp.exp(mine[i] - top) + other[i + 1] * jnp.exp(other[i] - top)]
    return jnp.stack(rows)


def outer_kernel(scale_ref, in_ref, out_ref, turned_ref, send_ref, keep_ref, wide_ref):
    q = in_ref.shape[0]
    half = send_ref.shape[0]

    @pl.when(pl.program_id(0) == 0)
    def _():
        for i in range(2):
            wide_ref[i] = jnp.broadcast_to(scale_ref[i:i + 1, :], (128, q)).T

    copies = in_ref.shape[1] // 128
    in_scale = jnp.concatenate([wide_ref[0]] * copies, axis=1)
    out_scale = jnp.concatenate([wide_ref[1]] * copies, axis=1)
    grad = (in_scale * in_ref[...] - out_scale * out_ref[...]).astype(BF)
    send_ref[...] = jnp.dot(turned_ref[:half, :], grad, preferred_element_type=F32).astype(BF)
    keep_ref[...] = jnp.dot(turned_ref[half:, :], grad, preferred_element_type=F32)


def outer(scales, in_sum, out_sum, turned):
    q, d = in_sum.shape
    f = turned.shape[0]
    tile = 256
    column = lambda i: (0, i)
    whole = lambda i: (0, 0)
    return pl.pallas_call(
        outer_kernel,
        out_shape=(jax.ShapeDtypeStruct((f // 2, d), BF), jax.ShapeDtypeStruct((f // 2, d), F32)),
        grid=(d // tile,),
        in_specs=[
            pl.BlockSpec((2, q), whole),
            pl.BlockSpec((q, tile), column),
            pl.BlockSpec((q, tile), column),
            pl.BlockSpec((f, q), whole),
        ],
        out_specs=[pl.BlockSpec((f // 2, tile), column), pl.BlockSpec((f // 2, tile), column)],
        scratch_shapes=[pltpu.VMEM((2, q, 128), F32)],
        compiler_params=pltpu.CompilerParams(vmem_limit_bytes=32 << 20),
        cost_estimate=pl.CostEstimate(flops=2 * q * f * d, bytes_accessed=8 * q * d, transcendentals=0),
        name="outer",
    )(scales, in_sum, out_sum, turned)


def body(features, head_weight, inliers, outliers, inlier_counts, outlier_counts, labels):
    n = lax.axis_size("cls")
    depth = lax.axis_size("batch")
    me = lax.axis_index("cls")
    core = me & 1
    d = head_weight.shape[1]
    half = d // 2
    links = list(range(1, n.bit_length() - 1))
    first, second = orders(links)

    to_first, to_second = scatter_masks(first), scatter_masks(second)
    to_place = me ^ by_core(core, [m ^ 1 for m in to_second] + to_first, [m ^ 1 for m in to_first] + to_second)
    turned = turn_features(features, to_place, n)

    pieces = jnp.stack([head_weight[:, :half], head_weight[:, half:]])
    own = lax.dynamic_index_in_dim(pieces, core, 0, keepdims=False)
    give = lax.dynamic_index_in_dim(pieces, 1 - core, 0, keepdims=False)
    blocks = jnp.concatenate([own, cls_swap(give, n, (0, 0))])
    for bit_of in zip(first, second):
        blocks = jnp.concatenate([blocks, cls_swap(blocks, n, bit_of)])
    from_place = me ^ by_core(core, gather_masks(first), gather_masks(second))
    mine = half_queries(features, blocks, from_place, n)
    other = cls_swap(mine, n, (0, 0))

    in_weights, out_weights, stats = local_weights(
        core.reshape(1), mine, other, inliers, outliers,
        inlier_counts.reshape(1, -1), outlier_counts.reshape(1, -1),
    )
    whole = stats
    for bit in range(n.bit_length() - 1):
        whole = merge(whole, cls_swap(whole, n, (bit, bit)))
    in_sum = jnp.dot(in_weights, inliers, preferred_element_type=F32)
    out_sum = jnp.dot(out_weights, outliers, preferred_element_type=F32)
    energy = ((whole[0] + jnp.log(whole[1])) - (whole[2] + jnp.log(whole[3]))) / beta
    label_sign = 2.0 * labels.astype(F32) - 1.0
    slope = -label_sign * jax.nn.sigmoid(-label_sign * energy)
    scales = jnp.stack([
        slope * jnp.exp(stats[0] - whole[0]) / whole[1],
        slope * jnp.exp(stats[2] - whole[2]) / whole[3],
    ])
    send, keep = outer(scales, in_sum, out_sum, turned)

    total = keep + cls_swap(send, n, (0, 0)).astype(F32)
    for bit_of in zip(first, second):
        middle = total.shape[0] // 2
        got = cls_swap(total[:middle].astype(BF), n, bit_of)
        total = total[middle:] + got.astype(F32)
    for bit_of in zip(*orders(list(range(depth.bit_length() - 1)))):
        sent = total.astype(BF)
        total = sent.astype(F32) + batch_swap(sent, n, depth, bit_of).astype(F32)
    return energy, total


def solution(mesh):
    placed = (
        P("batch", None),
        P("cls", None),
        P("cls", None),
        P("cls", None),
        P("cls"),
        P("cls"),
        P("batch"),
    )
    return jax.shard_map(
        body, mesh=mesh, in_specs=placed, out_specs=(P("batch"), P("cls", None)), check_vma=False
    )
```

```python
import functools

import jax
import jax.numpy as jnp
from jax import lax
from jax.experimental import pallas as pl
from jax.experimental.pallas import tpu as pltpu
from jax.sharding import PartitionSpec as P


beta = 2.0
BF = jnp.bfloat16
F32 = jnp.float32


def orders(bits):
    turn = len(bits) // 2
    return bits, bits[turn:] + bits[:turn]


def gather_masks(order):
    masks = [0]
    for bit in order:
        masks = masks + [mask ^ (1 << bit) for mask in masks]
    return masks


def scatter_masks(order):
    masks = [0]
    for bit in reversed(order):
        masks = [mask ^ (1 << bit) for mask in masks] + masks
    return masks


def by_core(core, first, second):
    return jnp.where(core == 0, jnp.array(first, jnp.int32), jnp.array(second, jnp.int32))


def cls_swap(value, n, bit_of):
    return lax.ppermute(value, "cls", [(i, i ^ (1 << bit_of[i & 1])) for i in range(n)])


def batch_swap(value, n, depth, bit_of):
    pairs = []
    for i in range(n):
        for j in range(depth):
            pairs.append((i * depth + j, i * depth + (j ^ (1 << bit_of[i & 1]))))
    return lax.ppermute(value, ("cls", "batch"), pairs)


def arrange_kernel(to_ref, from_ref, features_ref, turned_ref, early_ref, late_ref, whole_ref, lined_ref, *, n, rows):
    whole_ref[...] = features_ref[...].T
    for p in range(n):
        start = pl.multiple_of(to_ref[p] * rows, rows)
        turned_ref[p * rows:(p + 1) * rows, :] = whole_ref[pl.ds(start, rows), :]
        start = pl.multiple_of(from_ref[p] * rows, rows)
        lined_ref[p * rows:(p + 1) * rows, :] = whole_ref[pl.ds(start, rows), :]
    split = early_ref.shape[1]
    early_ref[...] = lined_ref[:split, :].T
    late_ref[...] = lined_ref[split:, :].T


def arrange(features, to_place, from_place, n):
    q, f = features.shape
    late = 2 * (f // n)
    vmem = pl.BlockSpec(memory_space=pltpu.VMEM)
    smem = pl.BlockSpec(memory_space=pltpu.SMEM)
    return pl.pallas_call(
        functools.partial(arrange_kernel, n=n, rows=f // n),
        out_shape=(
            jax.ShapeDtypeStruct((f, q), BF),
            jax.ShapeDtypeStruct((q, f - late), BF),
            jax.ShapeDtypeStruct((q, late), BF),
        ),
        in_specs=[smem, smem, vmem],
        out_specs=(vmem, vmem, vmem),
        scratch_shapes=[pltpu.VMEM((f, q), BF), pltpu.VMEM((f, q), BF)],
        compiler_params=pltpu.CompilerParams(vmem_limit_bytes=16 << 20),
        cost_estimate=pl.CostEstimate(flops=0, bytes_accessed=8 * q * f, transcendentals=0),
        name="arrange",
    )(to_place, from_place, features)


def early_kernel(features_ref, *refs, tile):
    *block_refs, out_ref, weight_ref = refs
    rows = block_refs[0].shape[0]
    for p, block_ref in enumerate(block_refs):
        weight_ref[p * rows:(p + 1) * rows, :] = block_ref[...]

    @pl.loop(0, features_ref.shape[0] // tile)
    def _(i):
        part = pl.ds(pl.multiple_of(i * tile, tile), tile)
        out_ref[part, :] = jnp.dot(features_ref[part, :], weight_ref[...], preferred_element_type=F32)


def early_queries(features, blocks):
    q, depth = features.shape
    d = blocks[0].shape[1]
    vmem = pl.BlockSpec(memory_space=pltpu.VMEM)
    return pl.pallas_call(
        functools.partial(early_kernel, tile=256),
        out_shape=jax.ShapeDtypeStruct((q, d), F32),
        in_specs=[vmem] * (1 + len(blocks)),
        out_specs=vmem,
        scratch_shapes=[pltpu.VMEM((depth, d), BF)],
        compiler_params=pltpu.CompilerParams(vmem_limit_bytes=16 << 20),
        cost_estimate=pl.CostEstimate(flops=2 * q * depth * d, bytes_accessed=4 * q * d, transcendentals=0),
        name="early",
    )(features, *blocks)


def to_rows(columns, width):
    r = columns[0].shape[0]
    lane = lax.broadcasted_iota(jnp.int32, (r, width), 1)
    mixed = jnp.broadcast_to(columns[0], (r, width))
    for i, column in enumerate(columns[1:], 1):
        mixed = jnp.where(lane == i, column, mixed)
    return mixed.T[: len(columns), :]


def score_kernel(part_ref, features_ref, mine_ref, other_ref, in_ref, out_ref, in_counts_ref, out_counts_ref,
                 in_weights_ref, out_weights_ref, stats_ref, weight_ref):
    rows = mine_ref.shape[0]

    @pl.when(pl.program_id(0) == 0)
    def _():
        weight_ref[:rows, :] = mine_ref[...]
        weight_ref[rows:, :] = other_ref[...]

    late = jnp.dot(features_ref[...], weight_ref[...], preferred_element_type=F32)
    queries = (part_ref[...] + late).astype(BF) * beta
    stats = []
    for patterns_ref, counts_ref, weights_ref in (
        (in_ref, in_counts_ref, in_weights_ref),
        (out_ref, out_counts_ref, out_weights_ref),
    ):
        scores = lax.dot_general(
            queries, patterns_ref[...], (((1,), (1,)), ((), ())), preferred_element_type=F32
        ) + jnp.log(counts_ref[...].astype(F32))
        top = jnp.max(scores, axis=1, keepdims=True)
        expon = jnp.exp(scores - top)
        weights_ref[...] = expon.astype(BF)
        stats += [top, jnp.sum(expon, axis=1, keepdims=True)]
    stats_ref[...] = to_rows(stats, 128)


def local_weights(part, features, mine, other, inliers, outliers, in_counts, out_counts):
    q, late = features.shape
    d = inliers.shape[1]
    tile = 256
    row = lambda i: (i, 0)
    whole = lambda i: (0, 0)
    ins, outs = inliers.shape[0], outliers.shape[0]
    return pl.pallas_call(
        score_kernel,
        out_shape=(
            jax.ShapeDtypeStruct((q, ins), BF),
            jax.ShapeDtypeStruct((q, outs), BF),
            jax.ShapeDtypeStruct((4, q), F32),
        ),
        grid=(q // tile,),
        in_specs=[
            pl.BlockSpec((tile, d), row),
            pl.BlockSpec((tile, late), row),
            pl.BlockSpec(mine.shape, whole),
            pl.BlockSpec(other.shape, whole),
            pl.BlockSpec((ins, d), whole),
            pl.BlockSpec((outs, d), whole),
            pl.BlockSpec((1, ins), whole),
            pl.BlockSpec((1, outs), whole),
        ],
        out_specs=[
            pl.BlockSpec((tile, ins), row),
            pl.BlockSpec((tile, outs), row),
            pl.BlockSpec((4, tile), lambda i: (0, i)),
        ],
        scratch_shapes=[pltpu.VMEM((late, d), BF)],
        compiler_params=pltpu.CompilerParams(vmem_limit_bytes=32 << 20),
        cost_estimate=pl.CostEstimate(
            flops=2 * q * d * (ins + outs), bytes_accessed=2 * d * (ins + outs), transcendentals=q * (ins + outs)
        ),
        name="scores",
    )(part, features, mine, other, inliers, outliers, in_counts, out_counts)


def merge(mine, other):
    rows = []
    for i in (0, 2):
        top = jnp.maximum(mine[i], other[i])
        rows += [top, mine[i + 1] * jnp.exp(mine[i] - top) + other[i + 1] * jnp.exp(other[i] - top)]
    return jnp.stack(rows)


def outer_kernel(scale_ref, in_ref, out_ref, turned_ref, send_ref, keep_ref, wide_ref):
    q = in_ref.shape[0]
    half = send_ref.shape[0]

    @pl.when(pl.program_id(0) == 0)
    def _():
        for i in range(2):
            wide_ref[i] = jnp.broadcast_to(scale_ref[i:i + 1, :], (128, q)).T

    copies = in_ref.shape[1] // 128
    in_scale = jnp.concatenate([wide_ref[0]] * copies, axis=1)
    out_scale = jnp.concatenate([wide_ref[1]] * copies, axis=1)
    grad = (in_scale * in_ref[...] - out_scale * out_ref[...]).astype(BF)
    send_ref[...] = jnp.dot(turned_ref[:half, :], grad, preferred_element_type=F32).astype(BF)
    keep_ref[...] = jnp.dot(turned_ref[half:, :], grad, preferred_element_type=F32)


def outer(scales, in_sum, out_sum, turned):
    q, d = in_sum.shape
    f = turned.shape[0]
    tile = 256
    column = lambda i: (0, i)
    whole = lambda i: (0, 0)
    return pl.pallas_call(
        outer_kernel,
        out_shape=(jax.ShapeDtypeStruct((f // 2, d), BF), jax.ShapeDtypeStruct((f // 2, d), F32)),
        grid=(d // tile,),
        in_specs=[
            pl.BlockSpec((2, q), whole),
            pl.BlockSpec((q, tile), column),
            pl.BlockSpec((q, tile), column),
            pl.BlockSpec((f, q), whole),
        ],
        out_specs=[pl.BlockSpec((f // 2, tile), column), pl.BlockSpec((f // 2, tile), column)],
        scratch_shapes=[pltpu.VMEM((2, q, 128), F32)],
        compiler_params=pltpu.CompilerParams(vmem_limit_bytes=32 << 20),
        cost_estimate=pl.CostEstimate(flops=2 * q * f * d, bytes_accessed=8 * q * d, transcendentals=0),
        name="outer",
    )(scales, in_sum, out_sum, turned)


def body(features, head_weight, inliers, outliers, inlier_counts, outlier_counts, labels):
    n = lax.axis_size("cls")
    depth = lax.axis_size("batch")
    me = lax.axis_index("cls")
    core = me & 1
    links = list(range(1, n.bit_length() - 1))
    first, second = orders(links)

    held = [head_weight]
    for bit_of in zip(first, second):
        for block in list(held):
            held.append(cls_swap(block, n, bit_of))
    swapped = []
    for block in held:
        swapped.append(cls_swap(block, n, (0, 0)))
    from_first, from_second = gather_masks(first), gather_masks(second)
    mine, other = (
        [masks[:-1] + [mask ^ 1 for mask in others[:-1]] + [masks[-1], others[-1] ^ 1]
         for masks, others in ((from_first, from_second), (from_second, from_first))]
    )
    from_place = me ^ by_core(core, mine, other)
    to_first, to_second = scatter_masks(first), scatter_masks(second)
    to_place = me ^ by_core(core, [m ^ 1 for m in to_second] + to_first, [m ^ 1 for m in to_first] + to_second)
    turned, early_features, late_features = arrange(features, to_place, from_place, n)

    part = early_queries(early_features, held[:-1] + swapped[:-1])
    in_weights, out_weights, stats = local_weights(
        part, late_features, held[-1], swapped[-1], inliers, outliers,
        inlier_counts.reshape(1, -1), outlier_counts.reshape(1, -1),
    )
    whole = stats
    for bit in range(n.bit_length() - 1):
        whole = merge(whole, cls_swap(whole, n, (bit, bit)))
    in_sum = jnp.dot(in_weights, inliers, preferred_element_type=F32)
    out_sum = jnp.dot(out_weights, outliers, preferred_element_type=F32)
    energy = ((whole[0] + jnp.log(whole[1])) - (whole[2] + jnp.log(whole[3]))) / beta
    label_sign = 2.0 * labels.astype(F32) - 1.0
    slope = -label_sign * jax.nn.sigmoid(-label_sign * energy)
    scales = jnp.stack([
        slope * jnp.exp(stats[0] - whole[0]) / whole[1],
        slope * jnp.exp(stats[2] - whole[2]) / whole[3],
    ])
    send, keep = outer(scales, in_sum, out_sum, turned)

    total = keep + cls_swap(send, n, (0, 0)).astype(F32)
    for bit_of in zip(first, second):
        middle = total.shape[0] // 2
        got = cls_swap(total[:middle].astype(BF), n, bit_of)
        total = total[middle:] + got.astype(F32)
    for bit_of in zip(*orders(list(range(depth.bit_length() - 1)))):
        sent = total.astype(BF)
        total = sent.astype(F32) + batch_swap(sent, n, depth, bit_of).astype(F32)
    return energy, total


def solution(mesh):
    placed = (
        P("batch", None),
        P("cls", None),
        P("cls", None),
        P("cls", None),
        P("cls"),
        P("cls"),
        P("batch"),
    )

    return jax.shard_map(body, mesh=mesh, in_specs=placed, out_specs=(P("batch"), P("cls", None)), check_vma=False)
```

```python
import functools

import jax
import jax.numpy as jnp
from jax import lax
from jax.experimental import pallas as pl
from jax.experimental.pallas import tpu as pltpu
from jax.sharding import PartitionSpec as P


beta = 2.0
BF = jnp.bfloat16
F32 = jnp.float32
PARTS = 2


def orders(bits):
    turn = len(bits) // 2
    return bits, bits[turn:] + bits[:turn]


def gather_masks(order):
    masks = [0]
    for bit in order:
        masks = masks + [mask ^ (1 << bit) for mask in masks]
    return masks


def scatter_masks(order):
    masks = [0]
    for bit in reversed(order):
        masks = [mask ^ (1 << bit) for mask in masks] + masks
    return masks


def position(me, masks, p):
    core = me & 1
    return me ^ (masks[0][p] + core * (masks[1][p] - masks[0][p]))


def cls_swap(value, n, bit_of):
    return lax.ppermute(value, "cls", [(i, i ^ (1 << bit_of[i & 1])) for i in range(n)])


def batch_swap(value, n, depth, bit_of):
    pairs = []
    for i in range(n):
        for j in range(depth):
            pairs.append((i * depth + j, i * depth + (j ^ (1 << bit_of[i & 1]))))
    return lax.ppermute(value, ("cls", "batch"), pairs)


def arrange_kernel(me_ref, features_ref, turned_ref, early_ref, late_ref, whole_ref, lined_ref,
                   *, to_masks, from_masks, rows):
    me = me_ref[0]
    whole_ref[...] = features_ref[...].T
    for p in range(len(to_masks[0])):
        start = pl.multiple_of(position(me, to_masks, p) * rows, rows)
        turned_ref[p * rows:(p + 1) * rows, :] = whole_ref[pl.ds(start, rows), :]
        start = pl.multiple_of(position(me, from_masks, p) * rows, rows)
        lined_ref[p * rows:(p + 1) * rows, :] = whole_ref[pl.ds(start, rows), :]
    split = early_ref.shape[1]
    early_ref[...] = lined_ref[:split, :].T
    late_ref[...] = lined_ref[split:, :].T


def arrange(features, me, to_masks, from_masks, n):
    q, f = features.shape
    late = 2 * (f // n)
    vmem = pl.BlockSpec(memory_space=pltpu.VMEM)
    smem = pl.BlockSpec(memory_space=pltpu.SMEM)
    return pl.pallas_call(
        functools.partial(arrange_kernel, to_masks=to_masks, from_masks=from_masks, rows=f // n),
        out_shape=(
            jax.ShapeDtypeStruct((f, q), BF),
            jax.ShapeDtypeStruct((q, f - late), BF),
            jax.ShapeDtypeStruct((q, late), BF),
        ),
        in_specs=[smem, vmem],
        out_specs=(vmem, vmem, vmem),
        scratch_shapes=[pltpu.VMEM((f, q), BF), pltpu.VMEM((f, q), BF)],
        compiler_params=pltpu.CompilerParams(vmem_limit_bytes=16 << 20),
        cost_estimate=pl.CostEstimate(flops=0, bytes_accessed=8 * q * f, transcendentals=0),
        name="arrange",
    )(me.reshape(1), features)


def early_kernel(features_ref, *refs, tile):
    *block_refs, out_ref, weight_ref = refs
    rows = block_refs[0].shape[0]
    for p, block_ref in enumerate(block_refs):
        weight_ref[p * rows:(p + 1) * rows, :] = block_ref[...]

    @pl.loop(0, features_ref.shape[0] // tile)
    def _(i):
        part = pl.ds(pl.multiple_of(i * tile, tile), tile)
        out_ref[part, :] = jnp.dot(features_ref[part, :], weight_ref[...], preferred_element_type=F32)


def early_queries(features, blocks):
    q, depth = features.shape
    d = blocks[0].shape[1]
    vmem = pl.BlockSpec(memory_space=pltpu.VMEM)
    return pl.pallas_call(
        functools.partial(early_kernel, tile=256),
        out_shape=jax.ShapeDtypeStruct((q, d), F32),
        in_specs=[vmem] * (1 + len(blocks)),
        out_specs=vmem,
        scratch_shapes=[pltpu.VMEM((depth, d), BF)],
        compiler_params=pltpu.CompilerParams(vmem_limit_bytes=16 << 20),
        cost_estimate=pl.CostEstimate(flops=2 * q * depth * d, bytes_accessed=4 * q * d, transcendentals=0),
        name="early",
    )(features, *blocks)


def to_rows(columns, width):
    r = columns[0].shape[0]
    lane = lax.broadcasted_iota(jnp.int32, (r, width), 1)
    mixed = jnp.broadcast_to(columns[0], (r, width))
    for i, column in enumerate(columns[1:], 1):
        mixed = jnp.where(lane == i, column, mixed)
    return mixed.T[: len(columns), :]


def score_kernel(part_ref, features_ref, mine_ref, other_ref, in_ref, out_ref, in_counts_ref, out_counts_ref,
                 in_weights_ref, out_weights_ref, stats_ref, weight_ref):
    rows = mine_ref.shape[0]

    @pl.when(pl.program_id(0) == 0)
    def _():
        weight_ref[:rows, :] = mine_ref[...]
        weight_ref[rows:, :] = other_ref[...]

    late = jnp.dot(features_ref[...], weight_ref[...], preferred_element_type=F32)
    queries = (part_ref[...] + late).astype(BF) * beta
    stats = []
    for patterns_ref, counts_ref, weights_ref in (
        (in_ref, in_counts_ref, in_weights_ref),
        (out_ref, out_counts_ref, out_weights_ref),
    ):
        scores = lax.dot_general(
            queries, patterns_ref[...], (((1,), (1,)), ((), ())), preferred_element_type=F32
        ) + jnp.log(counts_ref[...].astype(F32))
        top = jnp.max(scores, axis=1, keepdims=True)
        expon = jnp.exp(scores - top)
        weights_ref[...] = expon.astype(BF)
        stats += [top, jnp.sum(expon, axis=1, keepdims=True)]
    stats_ref[...] = to_rows(stats, 128)


def local_weights(part, features, mine, other, inliers, outliers, in_counts, out_counts):
    q, late = features.shape
    d = inliers.shape[1]
    tile = 256
    row = lambda i: (i, 0)
    whole = lambda i: (0, 0)
    ins, outs = inliers.shape[0], outliers.shape[0]
    return pl.pallas_call(
        score_kernel,
        out_shape=(
            jax.ShapeDtypeStruct((q, ins), BF),
            jax.ShapeDtypeStruct((q, outs), BF),
            jax.ShapeDtypeStruct((4, q), F32),
        ),
        grid=(q // tile,),
        in_specs=[
            pl.BlockSpec((tile, d), row),
            pl.BlockSpec((tile, late), row),
            pl.BlockSpec(mine.shape, whole),
            pl.BlockSpec(other.shape, whole),
            pl.BlockSpec((ins, d), whole),
            pl.BlockSpec((outs, d), whole),
            pl.BlockSpec((1, ins), whole),
            pl.BlockSpec((1, outs), whole),
        ],
        out_specs=[
            pl.BlockSpec((tile, ins), row),
            pl.BlockSpec((tile, outs), row),
            pl.BlockSpec((4, tile), lambda i: (0, i)),
        ],
        scratch_shapes=[pltpu.VMEM((late, d), BF)],
        compiler_params=pltpu.CompilerParams(vmem_limit_bytes=32 << 20),
        cost_estimate=pl.CostEstimate(
            flops=2 * q * d * (ins + outs), bytes_accessed=2 * d * (ins + outs), transcendentals=q * (ins + outs)
        ),
        name="scores",
    )(part, features, mine, other, inliers, outliers, in_counts, out_counts)


def merge(mine, other):
    rows = []
    for i in (0, 2):
        top = jnp.maximum(mine[i], other[i])
        rows += [top, mine[i + 1] * jnp.exp(mine[i] - top) + other[i + 1] * jnp.exp(other[i] - top)]
    return jnp.stack(rows)


def weigh_kernel(weights_ref, patterns_ref, out_ref):
    out_ref[...] = jnp.dot(weights_ref[...], patterns_ref[...], preferred_element_type=F32)


def weigh(weights, patterns, part, parts):
    q, count = weights.shape
    width = patterns.shape[1] // parts
    tile = 256
    return pl.pallas_call(
        weigh_kernel,
        out_shape=jax.ShapeDtypeStruct((q, width), F32),
        grid=(q // tile,),
        in_specs=[
            pl.BlockSpec((tile, count), lambda i: (i, 0)),
            pl.BlockSpec((count, width), lambda i: (0, part)),
        ],
        out_specs=pl.BlockSpec((tile, width), lambda i: (i, 0)),
        compiler_params=pltpu.CompilerParams(vmem_limit_bytes=16 << 20),
        cost_estimate=pl.CostEstimate(flops=2 * q * count * width, bytes_accessed=4 * q * width, transcendentals=0),
        name="weigh",
    )(weights, patterns)


def outer_kernel(scale_ref, in_ref, out_ref, turned_ref, send_ref, keep_ref, wide_ref):
    q = in_ref.shape[0]
    half = send_ref.shape[0]

    @pl.when(pl.program_id(0) == 0)
    def _():
        for i in range(2):
            wide_ref[i] = jnp.broadcast_to(scale_ref[i:i + 1, :], (128, q)).T

    copies = in_ref.shape[1] // 128
    in_scale = jnp.concatenate([wide_ref[0]] * copies, axis=1)
    out_scale = jnp.concatenate([wide_ref[1]] * copies, axis=1)
    grad = (in_scale * in_ref[...] - out_scale * out_ref[...]).astype(BF)
    send_ref[...] = jnp.dot(turned_ref[:half, :], grad, preferred_element_type=F32).astype(BF)
    keep_ref[...] = jnp.dot(turned_ref[half:, :], grad, preferred_element_type=F32)


def outer(scales, in_sum, out_sum, turned):
    q, d = in_sum.shape
    f = turned.shape[0]
    tile = 256
    column = lambda i: (0, i)
    whole = lambda i: (0, 0)
    return pl.pallas_call(
        outer_kernel,
        out_shape=(jax.ShapeDtypeStruct((f // 2, d), BF), jax.ShapeDtypeStruct((f // 2, d), F32)),
        grid=(d // tile,),
        in_specs=[
            pl.BlockSpec((2, q), whole),
            pl.BlockSpec((q, tile), column),
            pl.BlockSpec((q, tile), column),
            pl.BlockSpec((f, q), whole),
        ],
        out_specs=[pl.BlockSpec((f // 2, tile), column), pl.BlockSpec((f // 2, tile), column)],
        scratch_shapes=[pltpu.VMEM((2, q, 128), F32)],
        compiler_params=pltpu.CompilerParams(vmem_limit_bytes=24 << 20),
        cost_estimate=pl.CostEstimate(flops=2 * q * f * d, bytes_accessed=8 * q * d, transcendentals=0),
        name="outer",
    )(scales, in_sum, out_sum, turned)


def body(features, head_weight, inliers, outliers, inlier_counts, outlier_counts, labels):
    n = lax.axis_size("cls")
    depth = lax.axis_size("batch")
    me = lax.axis_index("cls")
    links = list(range(1, n.bit_length() - 1))
    first, second = orders(links)

    held = [head_weight]
    for bit_of in zip(first, second):
        for block in list(held):
            held.append(cls_swap(block, n, bit_of))
    swapped = []
    for block in held:
        swapped.append(cls_swap(block, n, (0, 0)))
    from_first, from_second = gather_masks(first), gather_masks(second)
    from_masks = [
        masks[:-1] + [mask ^ 1 for mask in others[:-1]] + [masks[-1], others[-1] ^ 1]
        for masks, others in ((from_first, from_second), (from_second, from_first))
    ]
    to_first, to_second = scatter_masks(first), scatter_masks(second)
    to_masks = [[m ^ 1 for m in to_second] + to_first, [m ^ 1 for m in to_first] + to_second]
    turned, early_features, late_features = arrange(features, me, to_masks, from_masks, n)

    part = early_queries(early_features, held[:-1] + swapped[:-1])
    in_weights, out_weights, stats = local_weights(
        part, late_features, held[-1], swapped[-1], inliers, outliers,
        inlier_counts.reshape(1, -1), outlier_counts.reshape(1, -1),
    )
    whole = stats
    for bit in range(n.bit_length() - 1):
        got = cls_swap(whole, n, (bit, bit))
        whole = merge(whole, got)
    sums = []
    for k in range(PARTS):
        pair = []
        for weights, patterns in ((in_weights, inliers), (out_weights, outliers)):
            pair.append(weigh(weights, patterns, k, PARTS))
        sums.append(pair)
    energy = ((whole[0] + jnp.log(whole[1])) - (whole[2] + jnp.log(whole[3]))) / beta
    label_sign = 2.0 * labels.astype(F32) - 1.0
    slope = -label_sign * jax.nn.sigmoid(-label_sign * energy)
    scales = jnp.stack([
        slope * jnp.exp(stats[0] - whole[0]) / whole[1],
        slope * jnp.exp(stats[2] - whole[2]) / whole[3],
    ])

    columns = []
    for in_sum, out_sum in sums:
        send, keep = outer(scales, in_sum, out_sum, turned)
        got = cls_swap(send, n, (0, 0))
        total = keep + got.astype(F32)
        for bit_of in zip(first, second):
            middle = total.shape[0] // 2
            sent = total[:middle].astype(BF)
            got = cls_swap(sent, n, bit_of)
            total = total[middle:] + got.astype(F32)
        for bit_of in zip(*orders(list(range(depth.bit_length() - 1)))):
            sent = total.astype(BF)
            got = batch_swap(sent, n, depth, bit_of)
            total = sent.astype(F32) + got.astype(F32)
        columns.append(total)
    return energy, jnp.concatenate(columns, axis=1)


def solution(mesh):
    placed = (
        P("batch", None),
        P("cls", None),
        P("cls", None),
        P("cls", None),
        P("cls"),
        P("cls"),
        P("batch"),
    )

    return jax.shard_map(body, mesh=mesh, in_specs=placed, out_specs=(P("batch"), P("cls", None)), check_vma=False)
```

```python
import functools
import math

import jax
import jax.numpy as jnp
from jax import lax
from jax.experimental import pallas as pl
from jax.experimental.pallas import tpu as pltpu
from jax.sharding import PartitionSpec as P


beta = 2.0
BF = jnp.bfloat16
F32 = jnp.float32
PARTS = 2


def orders(bits):
    turn = len(bits) // 2
    return bits, bits[turn:] + bits[:turn]


def gather_masks(order):
    masks = [0]
    for bit in order:
        masks = masks + [mask ^ (1 << bit) for mask in masks]
    return masks


def scatter_masks(order):
    masks = [0]
    for bit in reversed(order):
        masks = [mask ^ (1 << bit) for mask in masks] + masks
    return masks


def position(me, masks, p):
    core = me & 1
    return me ^ (masks[0][p] + core * (masks[1][p] - masks[0][p]))


def cls_swap(value, n, bit_of):
    return lax.ppermute(value, "cls", [(i, i ^ (1 << bit_of[i & 1])) for i in range(n)])


def batch_swap(value, n, depth, bit_of):
    pairs = []
    for i in range(n):
        for j in range(depth):
            pairs.append((i * depth + j, i * depth + (j ^ (1 << bit_of[i & 1]))))
    return lax.ppermute(value, ("cls", "batch"), pairs)


def arrange_kernel(me_ref, features_ref, turned_ref, early_ref, late_ref, whole_ref, lined_ref,
                   *, to_masks, from_masks, rows):
    me = me_ref[0]
    whole_ref[...] = features_ref[...].T
    for p in range(len(to_masks[0])):
        start = pl.multiple_of(position(me, to_masks, p) * rows, rows)
        turned_ref[p * rows:(p + 1) * rows, :] = whole_ref[pl.ds(start, rows), :]
        start = pl.multiple_of(position(me, from_masks, p) * rows, rows)
        lined_ref[p * rows:(p + 1) * rows, :] = whole_ref[pl.ds(start, rows), :]
    split = early_ref.shape[1]
    early_ref[...] = lined_ref[:split, :].T
    late_ref[...] = lined_ref[split:, :].T


def arrange(features, me, to_masks, from_masks, n):
    q, f = features.shape
    late = f // 2
    vmem = pl.BlockSpec(memory_space=pltpu.VMEM)
    smem = pl.BlockSpec(memory_space=pltpu.SMEM)
    return pl.pallas_call(
        functools.partial(arrange_kernel, to_masks=to_masks, from_masks=from_masks, rows=f // n),
        out_shape=(
            jax.ShapeDtypeStruct((f, q), BF),
            jax.ShapeDtypeStruct((q, f - late), BF),
            jax.ShapeDtypeStruct((q, late), BF),
        ),
        in_specs=[smem, vmem],
        out_specs=(vmem, vmem, vmem),
        scratch_shapes=[pltpu.VMEM((f, q), BF), pltpu.VMEM((f, q), BF)],
        compiler_params=pltpu.CompilerParams(vmem_limit_bytes=16 << 20),
        cost_estimate=pl.CostEstimate(flops=0, bytes_accessed=8 * q * f, transcendentals=0),
        name="arrange",
    )(me.reshape(1), features)


def join(block_refs, weight_ref):
    rows = block_refs[0].shape[0]
    for p, block_ref in enumerate(block_refs):
        weight_ref[p * rows:(p + 1) * rows, :] = block_ref[...]


def early_kernel(features_ref, *refs):
    *block_refs, out_ref, weight_ref = refs
    join(block_refs, weight_ref)
    out_ref[...] = jnp.dot(features_ref[...], weight_ref[...], preferred_element_type=F32)


def early_queries(features, blocks):
    q, depth = features.shape
    d = blocks[0].shape[1]
    vmem = pl.BlockSpec(memory_space=pltpu.VMEM)
    return pl.pallas_call(
        early_kernel,
        out_shape=jax.ShapeDtypeStruct((q, d), F32),
        in_specs=[vmem] * (1 + len(blocks)),
        out_specs=vmem,
        scratch_shapes=[pltpu.VMEM((depth, d), BF)],
        compiler_params=pltpu.CompilerParams(vmem_limit_bytes=16 << 20),
        cost_estimate=pl.CostEstimate(flops=2 * q * depth * d, bytes_accessed=4 * q * d, transcendentals=0),
        name="early",
    )(features, *blocks)


def to_rows(columns, width):
    r = columns[0].shape[0]
    lane = lax.broadcasted_iota(jnp.int32, (r, width), 1)
    mixed = jnp.broadcast_to(columns[0], (r, width))
    for i, column in enumerate(columns[1:], 1):
        mixed = jnp.where(lane == i, column, mixed)
    return mixed.T[: len(columns), :]


def score_kernel(part_ref, features_ref, in_ref, out_ref, in_counts_ref, out_counts_ref, *refs):
    *block_refs, in_weights_ref, out_weights_ref, stats_ref, weight_ref = refs

    @pl.when(pl.program_id(0) == 0)
    def _():
        join(block_refs, weight_ref)

    late = jnp.dot(features_ref[...], weight_ref[...], preferred_element_type=F32)
    queries = (part_ref[...] + late).astype(BF) * beta
    stats = []
    for patterns_ref, counts_ref, weights_ref in (
        (in_ref, in_counts_ref, in_weights_ref),
        (out_ref, out_counts_ref, out_weights_ref),
    ):
        scores = lax.dot_general(
            queries, patterns_ref[...], (((1,), (1,)), ((), ())), preferred_element_type=F32
        ) + jnp.log(counts_ref[...].astype(F32))
        top = jnp.max(scores, axis=1, keepdims=True)
        expon = jnp.exp(scores - top)
        weights_ref[...] = expon.astype(BF)
        stats += [top, jnp.sum(expon, axis=1, keepdims=True)]
    stats_ref[...] = to_rows(stats, 128)


def local_weights(part, features, blocks, inliers, outliers, in_counts, out_counts):
    q, late = features.shape
    d = inliers.shape[1]
    tile = math.gcd(q, 512)
    row = lambda i: (i, 0)
    whole = lambda i: (0, 0)
    ins, outs = inliers.shape[0], outliers.shape[0]
    return pl.pallas_call(
        score_kernel,
        out_shape=(
            jax.ShapeDtypeStruct((q, ins), BF),
            jax.ShapeDtypeStruct((q, outs), BF),
            jax.ShapeDtypeStruct((4, q), F32),
        ),
        grid=(q // tile,),
        in_specs=[
            pl.BlockSpec((tile, d), row),
            pl.BlockSpec((tile, late), row),
            pl.BlockSpec((ins, d), whole),
            pl.BlockSpec((outs, d), whole),
            pl.BlockSpec((1, ins), whole),
            pl.BlockSpec((1, outs), whole),
        ] + [pl.BlockSpec(block.shape, whole) for block in blocks],
        out_specs=[
            pl.BlockSpec((tile, ins), row),
            pl.BlockSpec((tile, outs), row),
            pl.BlockSpec((4, tile), lambda i: (0, i)),
        ],
        scratch_shapes=[pltpu.VMEM((late, d), BF)],
        compiler_params=pltpu.CompilerParams(vmem_limit_bytes=32 << 20),
        cost_estimate=pl.CostEstimate(
            flops=2 * q * d * (ins + outs), bytes_accessed=2 * d * (ins + outs), transcendentals=q * (ins + outs)
        ),
        name="scores",
    )(part, features, inliers, outliers, in_counts, out_counts, *blocks)


def merge(mine, other):
    rows = []
    for i in (0, 2):
        top = jnp.maximum(mine[i], other[i])
        rows += [top, mine[i + 1] * jnp.exp(mine[i] - top) + other[i + 1] * jnp.exp(other[i] - top)]
    return jnp.stack(rows)


def weigh_kernel(weights_ref, patterns_ref, out_ref):
    out_ref[...] = jnp.dot(weights_ref[...], patterns_ref[...], preferred_element_type=F32)


def weigh(weights, patterns, part, parts):
    q, count = weights.shape
    width = patterns.shape[1] // parts
    return pl.pallas_call(
        weigh_kernel,
        out_shape=jax.ShapeDtypeStruct((q, width), F32),
        grid=(1,),
        in_specs=[
            pl.BlockSpec((q, count), lambda i: (0, 0)),
            pl.BlockSpec((count, width), lambda i: (0, part)),
        ],
        out_specs=pl.BlockSpec((q, width), lambda i: (0, 0)),
        compiler_params=pltpu.CompilerParams(vmem_limit_bytes=16 << 20),
        cost_estimate=pl.CostEstimate(flops=2 * q * count * width, bytes_accessed=4 * q * width, transcendentals=0),
        name="weigh",
    )(weights, patterns)


def outer_kernel(scale_ref, in_ref, out_ref, turned_ref, send_ref, keep_ref):
    q, width = in_ref.shape
    half = send_ref.shape[0]
    copies = width // 128

    def wide(i):
        return jnp.concatenate([jnp.broadcast_to(scale_ref[i:i + 1, :], (128, q)).T] * copies, axis=1)

    grad = (wide(0) * in_ref[...] - wide(1) * out_ref[...]).astype(BF)
    send_ref[...] = jnp.dot(turned_ref[:half, :], grad, preferred_element_type=F32).astype(BF)
    keep_ref[...] = jnp.dot(turned_ref[half:, :], grad, preferred_element_type=F32)


def outer(scales, in_sum, out_sum, turned):
    q, width = in_sum.shape
    f = turned.shape[0]
    vmem = pl.BlockSpec(memory_space=pltpu.VMEM)
    return pl.pallas_call(
        outer_kernel,
        out_shape=(jax.ShapeDtypeStruct((f // 2, width), BF), jax.ShapeDtypeStruct((f // 2, width), F32)),
        in_specs=[vmem] * 4,
        out_specs=(vmem, vmem),
        compiler_params=pltpu.CompilerParams(vmem_limit_bytes=16 << 20),
        cost_estimate=pl.CostEstimate(flops=2 * q * f * width, bytes_accessed=8 * q * width, transcendentals=0),
        name="outer",
    )(scales, in_sum, out_sum, turned)


def body(features, head_weight, inliers, outliers, inlier_counts, outlier_counts, labels):
    n = lax.axis_size("cls")
    depth = lax.axis_size("batch")
    me = lax.axis_index("cls")
    links = list(range(1, n.bit_length() - 1))
    first, second = orders(links)

    held = [head_weight]
    for bit_of in zip(first, second):
        for block in list(held):
            held.append(cls_swap(block, n, bit_of))
    swapped = []
    for block in held:
        swapped.append(cls_swap(block, n, (0, 0)))
    from_first, from_second = gather_masks(first), gather_masks(second)
    early = n // 4
    from_masks = [
        masks[:early] + [mask ^ 1 for mask in others[:early]] + masks[early:] + [mask ^ 1 for mask in others[early:]]
        for masks, others in ((from_first, from_second), (from_second, from_first))
    ]
    to_first, to_second = scatter_masks(first), scatter_masks(second)
    to_masks = [[m ^ 1 for m in to_second] + to_first, [m ^ 1 for m in to_first] + to_second]
    turned, early_features, late_features = arrange(features, me, to_masks, from_masks, n)

    part = early_queries(early_features, held[:early] + swapped[:early])
    in_weights, out_weights, stats = local_weights(
        part, late_features, held[early:] + swapped[early:], inliers, outliers,
        inlier_counts.reshape(1, -1), outlier_counts.reshape(1, -1),
    )
    whole = stats
    for bit in range(n.bit_length() - 1):
        got = cls_swap(whole, n, (bit, bit))
        whole = merge(whole, got)
    sums = []
    for k in range(PARTS):
        pair = []
        for weights, patterns in ((in_weights, inliers), (out_weights, outliers)):
            pair.append(weigh(weights, patterns, k, PARTS))
        sums.append(pair)
    energy = ((whole[0] + jnp.log(whole[1])) - (whole[2] + jnp.log(whole[3]))) / beta
    label_sign = 2.0 * labels.astype(F32) - 1.0
    slope = -label_sign * jax.nn.sigmoid(-label_sign * energy)
    scales = jnp.stack([
        slope * jnp.exp(stats[0] - whole[0]) / whole[1],
        slope * jnp.exp(stats[2] - whole[2]) / whole[3],
    ])

    columns = []
    for in_sum, out_sum in sums:
        send, keep = outer(scales, in_sum, out_sum, turned)
        got = cls_swap(send, n, (0, 0))
        total = keep + got.astype(F32)
        for bit_of in zip(first, second):
            middle = total.shape[0] // 2
            sent = total[:middle].astype(BF)
            got = cls_swap(sent, n, bit_of)
            total = total[middle:] + got.astype(F32)
        for bit_of in zip(*orders(list(range(depth.bit_length() - 1)))):
            sent = total.astype(BF)
            got = batch_swap(sent, n, depth, bit_of)
            total = sent.astype(F32) + got.astype(F32)
        columns.append(total)
    return energy, jnp.concatenate(columns, axis=1)


def solution(mesh):
    placed = (
        P("batch", None),
        P("cls", None),
        P("cls", None),
        P("cls", None),
        P("cls"),
        P("cls"),
        P("batch"),
    )

    return jax.shard_map(body, mesh=mesh, in_specs=placed, out_specs=(P("batch"), P("cls", None)), check_vma=False)
```

```python
import functools
import math

import jax
import jax.numpy as jnp
from jax import lax
from jax.experimental import pallas as pl
from jax.experimental.pallas import tpu as pltpu
from jax.sharding import PartitionSpec as P


beta = 2.0
BF = jnp.bfloat16
F32 = jnp.float32
PARTS = 2


def orders(bits):
    turn = len(bits) // 2
    return bits, bits[turn:] + bits[:turn]


def gather_masks(order):
    masks = [0]
    for bit in order:
        masks = masks + [mask ^ (1 << bit) for mask in masks]
    return masks


def scatter_masks(order):
    masks = [0]
    for bit in reversed(order):
        masks = [mask ^ (1 << bit) for mask in masks] + masks
    return masks


def position(me, masks, p):
    core = me & 1
    return me ^ (masks[0][p] + core * (masks[1][p] - masks[0][p]))


def cls_swap(value, n, bit_of):
    return lax.ppermute(value, "cls", [(i, i ^ (1 << bit_of[i & 1])) for i in range(n)])


def batch_swap(value, n, depth, bit_of):
    pairs = []
    for i in range(n):
        for j in range(depth):
            pairs.append((i * depth + j, i * depth + (j ^ (1 << bit_of[i & 1]))))
    return lax.ppermute(value, ("cls", "batch"), pairs)


def turn_kernel(me_ref, features_ref, turned_ref, *refs, to_masks, from_masks, rows):
    me = me_ref[0]
    *lined_refs, whole_ref = refs
    whole_ref[...] = features_ref[...].T
    for masks, ref in ((to_masks, turned_ref), (from_masks, lined_refs[0] if lined_refs else None)):
        if ref is not None:
            for p in range(len(masks[0])):
                start = pl.multiple_of(position(me, masks, p) * rows, rows)
                ref[p * rows:(p + 1) * rows, :] = whole_ref[pl.ds(start, rows), :]


def turn(features, me, to_masks, from_masks, n, lined):
    q, f = features.shape
    vmem = pl.BlockSpec(memory_space=pltpu.VMEM)
    smem = pl.BlockSpec(memory_space=pltpu.SMEM)
    count = 2 if lined else 1
    return pl.pallas_call(
        functools.partial(turn_kernel, to_masks=to_masks, from_masks=from_masks, rows=f // n),
        out_shape=[jax.ShapeDtypeStruct((f, q), BF)] * count,
        in_specs=[smem, vmem],
        out_specs=[vmem] * count,
        scratch_shapes=[pltpu.VMEM((f, q), BF)],
        compiler_params=pltpu.CompilerParams(vmem_limit_bytes=16 << 20),
        cost_estimate=pl.CostEstimate(flops=0, bytes_accessed=8 * q * f, transcendentals=0),
        name="turn",
    )(me.reshape(1), features)


def join(block_refs, weight_ref):
    rows = block_refs[0].shape[0]
    for p, block_ref in enumerate(block_refs):
        weight_ref[p * rows:(p + 1) * rows, :] = block_ref[...]


def pick(me_ref, features_ref, picked_ref, masks, first, rows):
    if masks is None:
        return features_ref[:, first * rows:first * rows + picked_ref.shape[1]]
    for p in range(picked_ref.shape[1] // rows):
        start = pl.multiple_of(position(me_ref[0], masks, first + p) * rows, rows)
        picked_ref[:, p * rows:(p + 1) * rows] = features_ref[:, pl.ds(start, rows)]
    return picked_ref[...]


def part_kernel(me_ref, features_ref, *refs, masks, first, adds):
    *block_refs, out_ref, weight_ref, picked_ref = refs
    before_ref = block_refs.pop(0) if adds else None
    join(block_refs, weight_ref)
    columns = pick(me_ref, features_ref, picked_ref, masks, first, block_refs[0].shape[0])
    total = jnp.dot(columns, weight_ref[...], preferred_element_type=F32)
    out_ref[...] = before_ref[...] + total if adds else total


def query_part(me, features, blocks, masks, first, before):
    q = features.shape[0]
    rows, d = blocks[0].shape
    depth = rows * len(blocks)
    vmem = pl.BlockSpec(memory_space=pltpu.VMEM)
    return pl.pallas_call(
        functools.partial(part_kernel, masks=masks, first=first, adds=len(before)),
        out_shape=jax.ShapeDtypeStruct((q, d), F32),
        in_specs=[pl.BlockSpec(memory_space=pltpu.SMEM)] + [vmem] * (1 + len(before) + len(blocks)),
        out_specs=vmem,
        scratch_shapes=[pltpu.VMEM((depth, d), BF), pltpu.VMEM((q, depth), BF)],
        input_output_aliases={2: 0} if before else {},
        compiler_params=pltpu.CompilerParams(vmem_limit_bytes=16 << 20),
        cost_estimate=pl.CostEstimate(flops=2 * q * depth * d, bytes_accessed=4 * q * d, transcendentals=0),
        name="part",
    )(me.reshape(1), features, *before, *blocks)


def to_rows(columns, width):
    r = columns[0].shape[0]
    lane = lax.broadcasted_iota(jnp.int32, (r, width), 1)
    mixed = jnp.broadcast_to(columns[0], (r, width))
    for i, column in enumerate(columns[1:], 1):
        mixed = jnp.where(lane == i, column, mixed)
    return mixed.T[: len(columns), :]


def score_kernel(me_ref, part_ref, features_ref, in_ref, out_ref, in_counts_ref, out_counts_ref, *refs, masks):
    *block_refs, in_weights_ref, out_weights_ref, stats_ref, weight_ref, picked_ref = refs

    @pl.when(pl.program_id(0) == 0)
    def _():
        join(block_refs, weight_ref)

    rows = block_refs[0].shape[0]
    columns = pick(me_ref, features_ref, picked_ref, masks, features_ref.shape[1] // rows - len(block_refs), rows)
    late = jnp.dot(columns, weight_ref[...], preferred_element_type=F32)
    queries = (part_ref[...] + late).astype(BF) * beta
    stats = []
    for patterns_ref, counts_ref, weights_ref in (
        (in_ref, in_counts_ref, in_weights_ref),
        (out_ref, out_counts_ref, out_weights_ref),
    ):
        scores = lax.dot_general(
            queries, patterns_ref[...], (((1,), (1,)), ((), ())), preferred_element_type=F32
        ) + jnp.log(counts_ref[...].astype(F32))
        top = jnp.max(scores, axis=1, keepdims=True)
        expon = jnp.exp(scores - top)
        weights_ref[...] = expon.astype(BF)
        stats += [top, jnp.sum(expon, axis=1, keepdims=True)]
    stats_ref[...] = to_rows(stats, 128)


def local_weights(me, masks, part, features, blocks, inliers, outliers, in_counts, out_counts):
    q, f = features.shape
    late = sum(block.shape[0] for block in blocks)
    d = inliers.shape[1]
    tile = math.gcd(q, 512)
    row = lambda i: (i, 0)
    whole = lambda i: (0, 0)
    ins, outs = inliers.shape[0], outliers.shape[0]
    return pl.pallas_call(
        functools.partial(score_kernel, masks=masks),
        out_shape=(
            jax.ShapeDtypeStruct((q, ins), BF),
            jax.ShapeDtypeStruct((q, outs), BF),
            jax.ShapeDtypeStruct((4, q), F32),
        ),
        grid=(q // tile,),
        in_specs=[
            pl.BlockSpec(memory_space=pltpu.SMEM),
            pl.BlockSpec((tile, d), row),
            pl.BlockSpec((tile, f), row),
            pl.BlockSpec((ins, d), whole),
            pl.BlockSpec((outs, d), whole),
            pl.BlockSpec((1, ins), whole),
            pl.BlockSpec((1, outs), whole),
        ] + [pl.BlockSpec(block.shape, whole) for block in blocks],
        out_specs=[
            pl.BlockSpec((tile, ins), row),
            pl.BlockSpec((tile, outs), row),
            pl.BlockSpec((4, tile), lambda i: (0, i)),
        ],
        scratch_shapes=[pltpu.VMEM((late, d), BF), pltpu.VMEM((tile, late), BF)],
        compiler_params=pltpu.CompilerParams(vmem_limit_bytes=32 << 20),
        cost_estimate=pl.CostEstimate(
            flops=2 * q * d * (ins + outs), bytes_accessed=2 * d * (ins + outs), transcendentals=q * (ins + outs)
        ),
        name="scores",
    )(me.reshape(1), part, features, inliers, outliers, in_counts, out_counts, *blocks)


def merge(mine, other):
    rows = []
    for i in (0, 2):
        top = jnp.maximum(mine[i], other[i])
        rows += [top, mine[i + 1] * jnp.exp(mine[i] - top) + other[i + 1] * jnp.exp(other[i] - top)]
    return jnp.stack(rows)


def weigh_kernel(weights_ref, patterns_ref, out_ref, *, start):
    columns = patterns_ref[:, start:start + out_ref.shape[1]]
    out_ref[...] = jnp.dot(weights_ref[...], columns, preferred_element_type=F32)


def weigh(weights, patterns, start, width):
    q, count = weights.shape
    vmem = pl.BlockSpec(memory_space=pltpu.VMEM)
    return pl.pallas_call(
        functools.partial(weigh_kernel, start=start),
        out_shape=jax.ShapeDtypeStruct((q, width), F32),
        in_specs=[vmem, vmem],
        out_specs=vmem,
        compiler_params=pltpu.CompilerParams(vmem_limit_bytes=16 << 20),
        cost_estimate=pl.CostEstimate(flops=2 * q * count * width, bytes_accessed=4 * q * width, transcendentals=0),
        name="weigh",
    )(weights, patterns)


def outer_kernel(scale_ref, turned_ref, *refs):
    *sum_refs, grad_ref, send_ref = refs
    q = grad_ref.shape[0]
    half = send_ref.shape[0]
    wide = [jnp.broadcast_to(scale_ref[i:i + 1, :], (128, q)).T for i in range(2)]
    start = 0
    for in_ref, out_ref in zip(sum_refs[::2], sum_refs[1::2]):
        width = in_ref.shape[1]
        part = slice(start, start + width)
        in_scale, out_scale = (jnp.concatenate([scale] * (width // 128), axis=1) for scale in wide)
        grad = (in_scale * in_ref[...] - out_scale * out_ref[...]).astype(BF)
        grad_ref[:, part] = grad
        send_ref[:, part] = jnp.dot(turned_ref[:half, :], grad, preferred_element_type=F32).astype(BF)
        start += width


def outer(scales, turned, sums):
    f, q = turned.shape
    d = sum(value.shape[1] for value in sums[::2])
    vmem = pl.BlockSpec(memory_space=pltpu.VMEM)
    return pl.pallas_call(
        outer_kernel,
        out_shape=(jax.ShapeDtypeStruct((q, d), BF), jax.ShapeDtypeStruct((f // 2, d), BF)),
        in_specs=[vmem] * (2 + len(sums)),
        out_specs=(vmem, vmem),
        compiler_params=pltpu.CompilerParams(vmem_limit_bytes=20 << 20),
        cost_estimate=pl.CostEstimate(flops=q * f * d, bytes_accessed=8 * q * d, transcendentals=0),
        name="outer",
    )(scales, turned, *sums)


def keep_kernel(turned_ref, grad_ref, keep_ref):
    half = keep_ref.shape[0]
    keep_ref[...] = jnp.dot(turned_ref[half:, :], grad_ref[...], preferred_element_type=F32)


def outer_rest(turned, grad):
    f, q = turned.shape
    width = grad.shape[1]
    vmem = pl.BlockSpec(memory_space=pltpu.VMEM)
    return pl.pallas_call(
        keep_kernel,
        out_shape=jax.ShapeDtypeStruct((f // 2, width), F32),
        in_specs=[vmem] * 2,
        out_specs=vmem,
        compiler_params=pltpu.CompilerParams(vmem_limit_bytes=16 << 20),
        cost_estimate=pl.CostEstimate(flops=q * f * width, bytes_accessed=2 * f * width, transcendentals=0),
        name="rest",
    )(turned, grad)


def body(features, head_weight, inliers, outliers, inlier_counts, outlier_counts, labels):
    n = lax.axis_size("cls")
    depth = lax.axis_size("batch")
    me = lax.axis_index("cls")
    d = head_weight.shape[1]
    links = list(range(1, n.bit_length() - 1))
    first, second = orders(links)

    held = [head_weight]
    for bit_of in zip(first, second):
        for block in list(held):
            held.append(cls_swap(block, n, bit_of))
    swapped = []
    for block in held:
        swapped.append(cls_swap(block, n, (0, 0)))
    from_first, from_second = gather_masks(first), gather_masks(second)
    groups = [slice(0, n // 4), slice(n // 4, n // 2 - 1), slice(n // 2 - 1, n // 2)]
    from_masks = [
        [mask for group in groups for mask in masks[group] + [other ^ 1 for other in others[group]]]
        for masks, others in ((from_first, from_second), (from_second, from_first))
    ]
    to_first, to_second = scatter_masks(first), scatter_masks(second)
    to_masks = [[m ^ 1 for m in to_second] + to_first, [m ^ 1 for m in to_first] + to_second]
    rows = head_weight.shape[0]
    lined = rows % 128 != 0
    turned, *lines = turn(features, me, to_masks, from_masks, n, lined)
    read_masks = None if lined else from_masks
    columns = lines[0].T if lined else features

    sums, first_block = [], 0
    *before, last = [held[group] + swapped[group] for group in groups]
    for blocks in before:
        sums = [query_part(me, columns, blocks, read_masks, first_block, sums)]
        first_block += len(blocks)
    in_weights, out_weights, stats = local_weights(
        me, read_masks, sums[0], columns, last, inliers, outliers,
        inlier_counts.reshape(1, -1), outlier_counts.reshape(1, -1),
    )
    whole = stats
    for bit in range(n.bit_length() - 1):
        got = cls_swap(whole, n, (bit, bit))
        whole = merge(whole, got)
    sums, width = [], d // PARTS
    for k in range(PARTS):
        for weights, patterns in ((in_weights, inliers), (out_weights, outliers)):
            sums.append(weigh(weights, patterns, k * width, width))
    energy = ((whole[0] + jnp.log(whole[1])) - (whole[2] + jnp.log(whole[3]))) / beta
    label_sign = 2.0 * labels.astype(F32) - 1.0
    slope = -label_sign * jax.nn.sigmoid(-label_sign * energy)
    scales = jnp.stack([
        slope * jnp.exp(stats[0] - whole[0]) / whole[1],
        slope * jnp.exp(stats[2] - whole[2]) / whole[3],
    ])

    grad, send = outer(scales, turned, sums)
    got = cls_swap(send, n, (0, 0))
    keep = outer_rest(turned, grad)
    outputs = []
    for k in range(PARTS):
        part = slice(k * width, (k + 1) * width)
        total = keep[:, part] + got[:, part].astype(F32)
        for bit_of in zip(first, second):
            middle = total.shape[0] // 2
            sent = total[:middle].astype(BF)
            come = cls_swap(sent, n, bit_of)
            total = total[middle:] + come.astype(F32)
        for bit_of in zip(*orders(list(range(depth.bit_length() - 1)))):
            sent = total.astype(BF)
            come = batch_swap(sent, n, depth, bit_of)
            total = sent.astype(F32) + come.astype(F32)
        outputs.append(total)
    return energy, jnp.concatenate(outputs, axis=1)


def solution(mesh):
    placed = (
        P("batch", None),
        P("cls", None),
        P("cls", None),
        P("cls", None),
        P("cls"),
        P("cls"),
        P("batch"),
    )

    return jax.shard_map(body, mesh=mesh, in_specs=placed, out_specs=(P("batch"), P("cls", None)), check_vma=False)
```

```python
import functools
import math

import jax
import jax.numpy as jnp
from jax import lax
from jax.experimental import pallas as pl
from jax.experimental.pallas import tpu as pltpu
from jax.sharding import PartitionSpec as P


beta = 2.0
BF = jnp.bfloat16
F32 = jnp.float32
SHARES = (4, 4)


def orders(bits):
    turn = len(bits) // 2
    return bits, bits[turn:] + bits[:turn]


def gather_masks(order):
    masks = [0]
    for bit in order:
        masks = masks + [mask ^ (1 << bit) for mask in masks]
    return masks


def scatter_masks(order):
    masks = [0]
    for bit in reversed(order):
        masks = [mask ^ (1 << bit) for mask in masks] + masks
    return masks


def position(me, masks, p):
    core = me & 1
    return me ^ (masks[0][p] + core * (masks[1][p] - masks[0][p]))


def cls_swap(value, n, bit_of):
    return lax.ppermute(value, "cls", [(i, i ^ (1 << bit_of[i & 1])) for i in range(n)])


def batch_swap(value, n, depth, bit_of):
    pairs = []
    for i in range(n):
        for j in range(depth):
            pairs.append((i * depth + j, i * depth + (j ^ (1 << bit_of[i & 1]))))
    return lax.ppermute(value, ("cls", "batch"), pairs)


def turn_kernel(me_ref, features_ref, turned_ref, *refs, to_masks, from_masks, rows):
    me = me_ref[0]
    *lined_refs, whole_ref = refs
    whole_ref[...] = features_ref[...].T
    for masks, ref in ((to_masks, turned_ref), (from_masks, lined_refs[0] if lined_refs else None)):
        if ref is not None:
            for p in range(len(masks[0])):
                start = pl.multiple_of(position(me, masks, p) * rows, rows)
                ref[p * rows:(p + 1) * rows, :] = whole_ref[pl.ds(start, rows), :]


def turn(features, me, to_masks, from_masks, n, lined):
    q, f = features.shape
    vmem = pl.BlockSpec(memory_space=pltpu.VMEM)
    smem = pl.BlockSpec(memory_space=pltpu.SMEM)
    count = 2 if lined else 1
    return pl.pallas_call(
        functools.partial(turn_kernel, to_masks=to_masks, from_masks=from_masks, rows=f // n),
        out_shape=[jax.ShapeDtypeStruct((f, q), BF)] * count,
        in_specs=[smem, vmem],
        out_specs=[vmem] * count,
        scratch_shapes=[pltpu.VMEM((f, q), BF)],
        compiler_params=pltpu.CompilerParams(vmem_limit_bytes=16 << 20),
        cost_estimate=pl.CostEstimate(flops=0, bytes_accessed=8 * q * f, transcendentals=0),
        name="turn",
    )(me.reshape(1), features)


def join(block_refs, weight_ref):
    rows = block_refs[0].shape[0]
    for p, block_ref in enumerate(block_refs):
        weight_ref[p * rows:(p + 1) * rows, :] = block_ref[...]


def pick(me_ref, features_ref, picked_ref, masks, first, rows):
    if masks is None:
        return features_ref[:, first * rows:first * rows + picked_ref.shape[1]]
    for p in range(picked_ref.shape[1] // rows):
        start = pl.multiple_of(position(me_ref[0], masks, first + p) * rows, rows)
        picked_ref[:, p * rows:(p + 1) * rows] = features_ref[:, pl.ds(start, rows)]
    return picked_ref[...]


def part_kernel(me_ref, features_ref, *refs, masks, first, adds):
    *block_refs, out_ref, weight_ref, picked_ref = refs
    before_ref = block_refs.pop(0) if adds else None
    join(block_refs, weight_ref)
    columns = pick(me_ref, features_ref, picked_ref, masks, first, block_refs[0].shape[0])
    total = jnp.dot(columns, weight_ref[...], preferred_element_type=F32)
    out_ref[...] = before_ref[...] + total if adds else total


def query_part(me, features, blocks, masks, first, before):
    q = features.shape[0]
    rows, d = blocks[0].shape
    depth = rows * len(blocks)
    vmem = pl.BlockSpec(memory_space=pltpu.VMEM)
    return pl.pallas_call(
        functools.partial(part_kernel, masks=masks, first=first, adds=len(before)),
        out_shape=jax.ShapeDtypeStruct((q, d), F32),
        in_specs=[pl.BlockSpec(memory_space=pltpu.SMEM)] + [vmem] * (1 + len(before) + len(blocks)),
        out_specs=vmem,
        scratch_shapes=[pltpu.VMEM((depth, d), BF), pltpu.VMEM((q, depth), BF)],
        input_output_aliases={2: 0} if before else {},
        compiler_params=pltpu.CompilerParams(vmem_limit_bytes=16 << 20),
        cost_estimate=pl.CostEstimate(flops=2 * q * depth * d, bytes_accessed=4 * q * d, transcendentals=0),
        name="part",
    )(me.reshape(1), features, *before, *blocks)


def to_rows(columns, width):
    r = columns[0].shape[0]
    lane = lax.broadcasted_iota(jnp.int32, (r, width), 1)
    mixed = jnp.broadcast_to(columns[0], (r, width))
    for i, column in enumerate(columns[1:], 1):
        mixed = jnp.where(lane == i, column, mixed)
    return mixed.T[: len(columns), :]


def score_kernel(me_ref, part_ref, features_ref, in_ref, out_ref, in_counts_ref, out_counts_ref, *refs, masks):
    *block_refs, in_weights_ref, out_weights_ref, stats_ref, weight_ref, picked_ref = refs

    @pl.when(pl.program_id(0) == 0)
    def _():
        join(block_refs, weight_ref)

    rows = block_refs[0].shape[0]
    columns = pick(me_ref, features_ref, picked_ref, masks, features_ref.shape[1] // rows - len(block_refs), rows)
    late = jnp.dot(columns, weight_ref[...], preferred_element_type=F32)
    queries = (part_ref[...] + late).astype(BF) * beta
    stats = []
    for patterns_ref, counts_ref, weights_ref in (
        (in_ref, in_counts_ref, in_weights_ref),
        (out_ref, out_counts_ref, out_weights_ref),
    ):
        scores = lax.dot_general(
            queries, patterns_ref[...], (((1,), (1,)), ((), ())), preferred_element_type=F32
        ) + jnp.log(counts_ref[...].astype(F32))
        top = jnp.max(scores, axis=1, keepdims=True)
        expon = jnp.exp(scores - top)
        weights_ref[...] = expon.astype(BF)
        stats += [top, jnp.sum(expon, axis=1, keepdims=True)]
    stats_ref[...] = to_rows(stats, 128)


def local_weights(me, masks, part, features, blocks, inliers, outliers, in_counts, out_counts):
    q, f = features.shape
    late = sum(block.shape[0] for block in blocks)
    d = inliers.shape[1]
    tile = math.gcd(q, 512)
    row = lambda i: (i, 0)
    whole = lambda i: (0, 0)
    ins, outs = inliers.shape[0], outliers.shape[0]
    return pl.pallas_call(
        functools.partial(score_kernel, masks=masks),
        out_shape=(
            jax.ShapeDtypeStruct((q, ins), BF),
            jax.ShapeDtypeStruct((q, outs), BF),
            jax.ShapeDtypeStruct((4, q), F32),
        ),
        grid=(q // tile,),
        in_specs=[
            pl.BlockSpec(memory_space=pltpu.SMEM),
            pl.BlockSpec((tile, d), row),
            pl.BlockSpec((tile, f), row),
            pl.BlockSpec((ins, d), whole),
            pl.BlockSpec((outs, d), whole),
            pl.BlockSpec((1, ins), whole),
            pl.BlockSpec((1, outs), whole),
        ] + [pl.BlockSpec(block.shape, whole) for block in blocks],
        out_specs=[
            pl.BlockSpec((tile, ins), row),
            pl.BlockSpec((tile, outs), row),
            pl.BlockSpec((4, tile), lambda i: (0, i)),
        ],
        scratch_shapes=[pltpu.VMEM((late, d), BF), pltpu.VMEM((tile, late), BF)],
        compiler_params=pltpu.CompilerParams(vmem_limit_bytes=32 << 20),
        cost_estimate=pl.CostEstimate(
            flops=2 * q * d * (ins + outs), bytes_accessed=2 * d * (ins + outs), transcendentals=q * (ins + outs)
        ),
        name="scores",
    )(me.reshape(1), part, features, inliers, outliers, in_counts, out_counts, *blocks)


def merge(mine, other):
    rows = []
    for i in (0, 2):
        top = jnp.maximum(mine[i], other[i])
        rows += [top, mine[i + 1] * jnp.exp(mine[i] - top) + other[i + 1] * jnp.exp(other[i] - top)]
    return jnp.stack(rows)


def weigh_kernel(weights_ref, patterns_ref, out_ref, *, start):
    columns = patterns_ref[:, start:start + out_ref.shape[1]]
    out_ref[...] = jnp.dot(weights_ref[...], columns, preferred_element_type=F32)


def weigh(weights, patterns, start, width):
    q, count = weights.shape
    vmem = pl.BlockSpec(memory_space=pltpu.VMEM)
    return pl.pallas_call(
        functools.partial(weigh_kernel, start=start),
        out_shape=jax.ShapeDtypeStruct((q, width), F32),
        in_specs=[vmem, vmem],
        out_specs=vmem,
        compiler_params=pltpu.CompilerParams(vmem_limit_bytes=16 << 20),
        cost_estimate=pl.CostEstimate(flops=2 * q * count * width, bytes_accessed=4 * q * width, transcendentals=0),
        name="weigh",
    )(weights, patterns)


def outer_kernel(scale_ref, in_ref, out_ref, turned_ref, grad_ref, send_ref):
    q, width = in_ref.shape
    copies = width // 128

    def wide(i):
        return jnp.concatenate([jnp.broadcast_to(scale_ref[i:i + 1, :], (128, q)).T] * copies, axis=1)

    grad = (wide(0) * in_ref[...] - wide(1) * out_ref[...]).astype(BF)
    grad_ref[...] = grad
    half = send_ref.shape[0]
    send_ref[...] = jnp.dot(turned_ref[:half, :], grad, preferred_element_type=F32).astype(BF)


def outer(scales, in_sum, out_sum, turned):
    q, width = in_sum.shape
    f = turned.shape[0]
    vmem = pl.BlockSpec(memory_space=pltpu.VMEM)
    return pl.pallas_call(
        outer_kernel,
        out_shape=(jax.ShapeDtypeStruct((q, width), BF), jax.ShapeDtypeStruct((f // 2, width), BF)),
        in_specs=[vmem] * 4,
        out_specs=(vmem, vmem),
        compiler_params=pltpu.CompilerParams(vmem_limit_bytes=16 << 20),
        cost_estimate=pl.CostEstimate(flops=q * f * width, bytes_accessed=8 * q * width, transcendentals=0),
        name="outer",
    )(scales, in_sum, out_sum, turned)


def keep_kernel(turned_ref, grad_ref, keep_ref):
    half = keep_ref.shape[0]
    keep_ref[...] = jnp.dot(turned_ref[half:, :], grad_ref[...], preferred_element_type=F32)


def outer_rest(turned, grad):
    f, q = turned.shape
    width = grad.shape[1]
    vmem = pl.BlockSpec(memory_space=pltpu.VMEM)
    return pl.pallas_call(
        keep_kernel,
        out_shape=jax.ShapeDtypeStruct((f // 2, width), F32),
        in_specs=[vmem] * 2,
        out_specs=vmem,
        compiler_params=pltpu.CompilerParams(vmem_limit_bytes=16 << 20),
        cost_estimate=pl.CostEstimate(flops=q * f * width, bytes_accessed=2 * f * width, transcendentals=0),
        name="rest",
    )(turned, grad)


def body(features, head_weight, inliers, outliers, inlier_counts, outlier_counts, labels):
    n = lax.axis_size("cls")
    depth = lax.axis_size("batch")
    me = lax.axis_index("cls")
    d = head_weight.shape[1]
    links = list(range(1, n.bit_length() - 1))
    first, second = orders(links)

    held = [head_weight]
    for bit_of in zip(first, second):
        for block in list(held):
            held.append(cls_swap(block, n, bit_of))
    swapped = []
    for block in held:
        swapped.append(cls_swap(block, n, (0, 0)))
    from_first, from_second = gather_masks(first), gather_masks(second)
    groups = [slice(0, n // 4), slice(n // 4, n // 2 - 1), slice(n // 2 - 1, n // 2)]
    from_masks = [
        [mask for group in groups for mask in masks[group] + [other ^ 1 for other in others[group]]]
        for masks, others in ((from_first, from_second), (from_second, from_first))
    ]
    to_first, to_second = scatter_masks(first), scatter_masks(second)
    to_masks = [[m ^ 1 for m in to_second] + to_first, [m ^ 1 for m in to_first] + to_second]
    rows = head_weight.shape[0]
    lined = rows % 128 != 0
    turned, *lines = turn(features, me, to_masks, from_masks, n, lined)
    read_masks = None if lined else from_masks
    columns = lines[0].T if lined else features

    sums, first_block = [], 0
    *before, last = [held[group] + swapped[group] for group in groups]
    for blocks in before:
        sums = [query_part(me, columns, blocks, read_masks, first_block, sums)]
        first_block += len(blocks)
    in_weights, out_weights, stats = local_weights(
        me, read_masks, sums[0], columns, last, inliers, outliers,
        inlier_counts.reshape(1, -1), outlier_counts.reshape(1, -1),
    )
    whole = stats
    for bit in list(range(1, n.bit_length() - 1)) + [0]:
        got = cls_swap(whole, n, (bit, bit))
        whole = merge(whole, got)
    sums = []
    widths = [share * d // 8 for share in SHARES]
    for k, width in enumerate(widths):
        pair = []
        for weights, patterns in ((in_weights, inliers), (out_weights, outliers)):
            pair.append(weigh(weights, patterns, sum(widths[:k]), width))
        sums.append(pair)
    energy = ((whole[0] + jnp.log(whole[1])) - (whole[2] + jnp.log(whole[3]))) / beta
    label_sign = 2.0 * labels.astype(F32) - 1.0
    slope = -label_sign * jax.nn.sigmoid(-label_sign * energy)
    scales = jnp.stack([
        slope * jnp.exp(stats[0] - whole[0]) / whole[1],
        slope * jnp.exp(stats[2] - whole[2]) / whole[3],
    ])

    columns = []
    for in_sum, out_sum in sums:
        grad, send = outer(scales, in_sum, out_sum, turned)
        got = cls_swap(send, n, (0, 0))
        keep = outer_rest(turned, grad)
        total = keep + got.astype(F32)
        for bit_of in zip(first, second):
            middle = total.shape[0] // 2
            sent = total[:middle].astype(BF)
            got = cls_swap(sent, n, bit_of)
            total = total[middle:] + got.astype(F32)
        for bit_of in zip(*orders(list(range(depth.bit_length() - 1)))):
            sent = total.astype(BF)
            got = batch_swap(sent, n, depth, bit_of)
            total = sent.astype(F32) + got.astype(F32)
        columns.append(total)
    return energy, jnp.concatenate(columns, axis=1)


def solution(mesh):
    placed = (
        P("batch", None),
        P("cls", None),
        P("cls", None),
        P("cls", None),
        P("cls"),
        P("cls"),
        P("batch"),
    )

    return jax.shard_map(body, mesh=mesh, in_specs=placed, out_specs=(P("batch"), P("cls", None)), check_vma=False)
```

```python
import functools
import math

import jax
import jax.numpy as jnp
from jax import lax
from jax.experimental import pallas as pl
from jax.experimental.pallas import tpu as pltpu
from jax.sharding import PartitionSpec as P


beta = 2.0
BF = jnp.bfloat16
F32 = jnp.float32
SHARES = (4, 4)


def orders(bits):
    turn = len(bits) // 2
    return bits, bits[turn:] + bits[:turn]


def gather_masks(order):
    masks = [0]
    for bit in order:
        masks = masks + [mask ^ (1 << bit) for mask in masks]
    return masks


def scatter_masks(order):
    masks = [0]
    for bit in reversed(order):
        masks = [mask ^ (1 << bit) for mask in masks] + masks
    return masks


def position(me, masks, p):
    core = me & 1
    return me ^ (masks[0][p] + core * (masks[1][p] - masks[0][p]))


def cls_swap(value, n, bit_of):
    return lax.ppermute(value, "cls", [(i, i ^ (1 << bit_of[i & 1])) for i in range(n)])


def batch_swap(value, n, depth, bit_of):
    pairs = []
    for i in range(n):
        for j in range(depth):
            pairs.append((i * depth + j, i * depth + (j ^ (1 << bit_of[i & 1]))))
    return lax.ppermute(value, ("cls", "batch"), pairs)


def turn_kernel(me_ref, features_ref, turned_ref, *refs, to_masks, from_masks, rows):
    me = me_ref[0]
    *lined_refs, whole_ref = refs
    whole_ref[...] = features_ref[...].T
    for masks, ref in ((to_masks, turned_ref), (from_masks, lined_refs[0] if lined_refs else None)):
        if ref is not None:
            for p in range(len(masks[0])):
                start = pl.multiple_of(position(me, masks, p) * rows, rows)
                ref[p * rows:(p + 1) * rows, :] = whole_ref[pl.ds(start, rows), :]


def turn(features, me, to_masks, from_masks, n, lined):
    q, f = features.shape
    vmem = pl.BlockSpec(memory_space=pltpu.VMEM)
    smem = pl.BlockSpec(memory_space=pltpu.SMEM)
    count = 2 if lined else 1
    return pl.pallas_call(
        functools.partial(turn_kernel, to_masks=to_masks, from_masks=from_masks, rows=f // n),
        out_shape=[jax.ShapeDtypeStruct((f, q), BF)] * count,
        in_specs=[smem, vmem],
        out_specs=[vmem] * count,
        scratch_shapes=[pltpu.VMEM((f, q), BF)],
        compiler_params=pltpu.CompilerParams(vmem_limit_bytes=16 << 20),
        cost_estimate=pl.CostEstimate(flops=0, bytes_accessed=8 * q * f, transcendentals=0),
        name="turn",
    )(me.reshape(1), features)


def join(block_refs, weight_ref):
    rows = block_refs[0].shape[0]
    for p, block_ref in enumerate(block_refs):
        weight_ref[p * rows:(p + 1) * rows, :] = block_ref[...]


def pick(me_ref, features_ref, picked_ref, masks, first, rows):
    if masks is None:
        return features_ref[:, first * rows:first * rows + picked_ref.shape[1]]
    for p in range(picked_ref.shape[1] // rows):
        start = pl.multiple_of(position(me_ref[0], masks, first + p) * rows, rows)
        picked_ref[:, p * rows:(p + 1) * rows] = features_ref[:, pl.ds(start, rows)]
    return picked_ref[...]


def part_kernel(me_ref, features_ref, *refs, masks, first, adds):
    *block_refs, out_ref, weight_ref, picked_ref = refs
    before_ref = block_refs.pop(0) if adds else None
    join(block_refs, weight_ref)
    columns = pick(me_ref, features_ref, picked_ref, masks, first, block_refs[0].shape[0])
    total = jnp.dot(columns, weight_ref[...], preferred_element_type=F32)
    out_ref[...] = before_ref[...] + total if adds else total


def query_part(me, features, blocks, masks, first, before):
    q = features.shape[0]
    rows, d = blocks[0].shape
    depth = rows * len(blocks)
    vmem = pl.BlockSpec(memory_space=pltpu.VMEM)
    return pl.pallas_call(
        functools.partial(part_kernel, masks=masks, first=first, adds=len(before)),
        out_shape=jax.ShapeDtypeStruct((q, d), F32),
        in_specs=[pl.BlockSpec(memory_space=pltpu.SMEM)] + [vmem] * (1 + len(before) + len(blocks)),
        out_specs=vmem,
        scratch_shapes=[pltpu.VMEM((depth, d), BF), pltpu.VMEM((q, depth), BF)],
        input_output_aliases={2: 0} if before else {},
        compiler_params=pltpu.CompilerParams(vmem_limit_bytes=16 << 20),
        cost_estimate=pl.CostEstimate(flops=2 * q * depth * d, bytes_accessed=4 * q * d, transcendentals=0),
        name="part",
    )(me.reshape(1), features, *before, *blocks)


def to_rows(columns, width):
    r = columns[0].shape[0]
    lane = lax.broadcasted_iota(jnp.int32, (r, width), 1)
    mixed = jnp.broadcast_to(columns[0], (r, width))
    for i, column in enumerate(columns[1:], 1):
        mixed = jnp.where(lane == i, column, mixed)
    return mixed.T[: len(columns), :]


def score_kernel(me_ref, part_ref, features_ref, in_ref, out_ref, in_counts_ref, out_counts_ref, *refs, masks):
    *block_refs, in_weights_ref, out_weights_ref, stats_ref, weight_ref, picked_ref = refs

    @pl.when(pl.program_id(0) == 0)
    def _():
        join(block_refs, weight_ref)

    rows = block_refs[0].shape[0]
    columns = pick(me_ref, features_ref, picked_ref, masks, features_ref.shape[1] // rows - len(block_refs), rows)
    late = jnp.dot(columns, weight_ref[...], preferred_element_type=F32)
    queries = (part_ref[...] + late).astype(BF) * beta
    sets = (
        (in_ref, in_counts_ref, in_weights_ref),
        (out_ref, out_counts_ref, out_weights_ref),
    )
    products = [
        lax.dot_general(queries, patterns_ref[...], (((1,), (1,)), ((), ())), preferred_element_type=F32)
        for patterns_ref, _, _ in sets
    ]
    stats = []
    for product, (_, counts_ref, weights_ref) in zip(products, sets):
        scores = product + jnp.log(counts_ref[...].astype(F32))
        top = jnp.max(scores, axis=1, keepdims=True)
        expon = jnp.exp(scores - top)
        weights_ref[...] = expon.astype(BF)
        stats += [top, jnp.sum(expon, axis=1, keepdims=True)]
    stats_ref[...] = to_rows(stats, 128)


def local_weights(me, masks, part, features, blocks, inliers, outliers, in_counts, out_counts):
    q, f = features.shape
    late = sum(block.shape[0] for block in blocks)
    d = inliers.shape[1]
    tile = math.gcd(q, 512)
    row = lambda i: (i, 0)
    whole = lambda i: (0, 0)
    ins, outs = inliers.shape[0], outliers.shape[0]
    return pl.pallas_call(
        functools.partial(score_kernel, masks=masks),
        out_shape=(
            jax.ShapeDtypeStruct((q, ins), BF),
            jax.ShapeDtypeStruct((q, outs), BF),
            jax.ShapeDtypeStruct((4, q), F32),
        ),
        grid=(q // tile,),
        in_specs=[
            pl.BlockSpec(memory_space=pltpu.SMEM),
            pl.BlockSpec((tile, d), row),
            pl.BlockSpec((tile, f), row),
            pl.BlockSpec((ins, d), whole),
            pl.BlockSpec((outs, d), whole),
            pl.BlockSpec((1, ins), whole),
            pl.BlockSpec((1, outs), whole),
        ] + [pl.BlockSpec(block.shape, whole) for block in blocks],
        out_specs=[
            pl.BlockSpec((tile, ins), row),
            pl.BlockSpec((tile, outs), row),
            pl.BlockSpec((4, tile), lambda i: (0, i)),
        ],
        scratch_shapes=[pltpu.VMEM((late, d), BF), pltpu.VMEM((tile, late), BF)],
        compiler_params=pltpu.CompilerParams(vmem_limit_bytes=32 << 20),
        cost_estimate=pl.CostEstimate(
            flops=2 * q * d * (ins + outs), bytes_accessed=2 * d * (ins + outs), transcendentals=q * (ins + outs)
        ),
        name="scores",
    )(me.reshape(1), part, features, inliers, outliers, in_counts, out_counts, *blocks)


def merge(mine, other):
    rows = []
    for i in (0, 2):
        top = jnp.maximum(mine[i], other[i])
        rows += [top, mine[i + 1] * jnp.exp(mine[i] - top) + other[i + 1] * jnp.exp(other[i] - top)]
    return jnp.stack(rows)


def weigh_kernel(weights_ref, patterns_ref, out_ref, *, start):
    columns = patterns_ref[:, start:start + out_ref.shape[1]]
    out_ref[...] = jnp.dot(weights_ref[...], columns, preferred_element_type=F32)


def weigh(weights, patterns, start, width):
    q, count = weights.shape
    vmem = pl.BlockSpec(memory_space=pltpu.VMEM)
    return pl.pallas_call(
        functools.partial(weigh_kernel, start=start),
        out_shape=jax.ShapeDtypeStruct((q, width), F32),
        in_specs=[vmem, vmem],
        out_specs=vmem,
        compiler_params=pltpu.CompilerParams(vmem_limit_bytes=16 << 20),
        cost_estimate=pl.CostEstimate(flops=2 * q * count * width, bytes_accessed=4 * q * width, transcendentals=0),
        name="weigh",
    )(weights, patterns)


def outer_kernel(scale_ref, in_ref, out_ref, turned_ref, grad_ref, send_ref):
    q, width = in_ref.shape
    copies = width // 128

    def wide(i):
        return jnp.concatenate([jnp.broadcast_to(scale_ref[i:i + 1, :], (128, q)).T] * copies, axis=1)

    grad = (wide(0) * in_ref[...] - wide(1) * out_ref[...]).astype(BF)
    grad_ref[...] = grad
    half = send_ref.shape[0]
    send_ref[...] = jnp.dot(turned_ref[:half, :], grad, preferred_element_type=F32).astype(BF)


def outer(scales, in_sum, out_sum, turned):
    q, width = in_sum.shape
    f = turned.shape[0]
    vmem = pl.BlockSpec(memory_space=pltpu.VMEM)
    return pl.pallas_call(
        outer_kernel,
        out_shape=(jax.ShapeDtypeStruct((q, width), BF), jax.ShapeDtypeStruct((f // 2, width), BF)),
        in_specs=[vmem] * 4,
        out_specs=(vmem, vmem),
        compiler_params=pltpu.CompilerParams(vmem_limit_bytes=16 << 20),
        cost_estimate=pl.CostEstimate(flops=q * f * width, bytes_accessed=8 * q * width, transcendentals=0),
        name="outer",
    )(scales, in_sum, out_sum, turned)


def keep_kernel(turned_ref, grad_ref, keep_ref):
    half = keep_ref.shape[0]
    keep_ref[...] = jnp.dot(turned_ref[half:, :], grad_ref[...], preferred_element_type=F32)


def outer_rest(turned, grad):
    f, q = turned.shape
    width = grad.shape[1]
    vmem = pl.BlockSpec(memory_space=pltpu.VMEM)
    return pl.pallas_call(
        keep_kernel,
        out_shape=jax.ShapeDtypeStruct((f // 2, width), F32),
        in_specs=[vmem] * 2,
        out_specs=vmem,
        compiler_params=pltpu.CompilerParams(vmem_limit_bytes=16 << 20),
        cost_estimate=pl.CostEstimate(flops=q * f * width, bytes_accessed=2 * f * width, transcendentals=0),
        name="rest",
    )(turned, grad)


def body(features, head_weight, inliers, outliers, inlier_counts, outlier_counts, labels):
    n = lax.axis_size("cls")
    depth = lax.axis_size("batch")
    me = lax.axis_index("cls")
    d = head_weight.shape[1]
    links = list(range(1, n.bit_length() - 1))
    first, second = orders(links)

    held = [head_weight]
    for bit_of in zip(first, second):
        for block in list(held):
            held.append(cls_swap(block, n, bit_of))
    swapped = []
    for block in held:
        swapped.append(cls_swap(block, n, (0, 0)))
    from_first, from_second = gather_masks(first), gather_masks(second)
    groups = [slice(0, n // 4), slice(n // 4, n // 2 - 1), slice(n // 2 - 1, n // 2)]
    from_masks = [
        [mask for group in groups for mask in masks[group] + [other ^ 1 for other in others[group]]]
        for masks, others in ((from_first, from_second), (from_second, from_first))
    ]
    to_first, to_second = scatter_masks(first), scatter_masks(second)
    to_masks = [[m ^ 1 for m in to_second] + to_first, [m ^ 1 for m in to_first] + to_second]
    rows = head_weight.shape[0]
    lined = rows % 128 != 0
    turned, *lines = turn(features, me, to_masks, from_masks, n, lined)
    read_masks = None if lined else from_masks
    columns = lines[0].T if lined else features

    sums, first_block = [], 0
    *before, last = [held[group] + swapped[group] for group in groups]
    for blocks in before:
        sums = [query_part(me, columns, blocks, read_masks, first_block, sums)]
        first_block += len(blocks)
    in_weights, out_weights, stats = local_weights(
        me, read_masks, sums[0], columns, last, inliers, outliers,
        inlier_counts.reshape(1, -1), outlier_counts.reshape(1, -1),
    )
    whole = stats
    for bit in list(range(1, n.bit_length() - 1)) + [0]:
        got = cls_swap(whole, n, (bit, bit))
        whole = merge(whole, got)
    sums = []
    widths = [share * d // 8 for share in SHARES]
    for k, width in enumerate(widths):
        pair = []
        for weights, patterns in ((in_weights, inliers), (out_weights, outliers)):
            pair.append(weigh(weights, patterns, sum(widths[:k]), width))
        sums.append(pair)
    energy = ((whole[0] + jnp.log(whole[1])) - (whole[2] + jnp.log(whole[3]))) / beta
    label_sign = 2.0 * labels.astype(F32) - 1.0
    slope = -label_sign * jax.nn.sigmoid(-label_sign * energy)
    scales = jnp.stack([
        slope * jnp.exp(stats[0] - whole[0]) / whole[1],
        slope * jnp.exp(stats[2] - whole[2]) / whole[3],
    ])

    columns = []
    for in_sum, out_sum in sums:
        grad, send = outer(scales, in_sum, out_sum, turned)
        got = cls_swap(send, n, (0, 0))
        keep = outer_rest(turned, grad)
        total = keep + got.astype(F32)
        for bit_of in zip(first, second):
            middle = total.shape[0] // 2
            sent = total[:middle].astype(BF)
            got = cls_swap(sent, n, bit_of)
            total = total[middle:] + got.astype(F32)
        for bit_of in zip(*orders(list(range(depth.bit_length() - 1)))):
            sent = total.astype(BF)
            got = batch_swap(sent, n, depth, bit_of)
            total = sent.astype(F32) + got.astype(F32)
        columns.append(total)
    return energy, jnp.concatenate(columns, axis=1)


def solution(mesh):
    placed = (
        P("batch", None),
        P("cls", None),
        P("cls", None),
        P("cls", None),
        P("cls"),
        P("cls"),
        P("batch"),
    )

    return jax.shard_map(body, mesh=mesh, in_specs=placed, out_specs=(P("batch"), P("cls", None)), check_vma=False)
```
